32 devices in a mesh: grp: 2 (over y), ja: 4 (over z), ia: 4 (over x, core).
Axes of the slice: x: 2, y: 2, z: 4, core: 2. Of those that a mesh axis runs over, the one named last changes fastest.
Arguments:
- pos_vel: float32 [6, 8192], P(None, ('grp', 'ja')), parts along dimension 1, may hold values from -6 to 6
- acc_jerk: float32 [6, 8192], P(None, ('grp', 'ja')), parts along dimension 1, may hold values from -6 to 6
- mass: float32 [8192], P(('grp', 'ja')), parts along dimension 0, may hold values from 7.324219e-05 to 0.0007324219
- age: float32 [8192], P(('grp', 'ja')), parts along dimension 0, may hold values from 0.125 to 0.5
- active_local: int32 [12288], P(('grp', 'ia')), parts along dimension 0, may hold values from 0 to 1023
- active_owner: int32 [12288], P(('grp', 'ia')), parts along dimension 0, may hold values from 0 to 3
Outputs:
- state: float32 [6, 12288], P(None, ('grp', 'ia')), parts along dimension 1
- forces: float32 [7, 12288], P(None, ('grp', 'ia')), parts along dimension 1
The draws below stay inside these ranges and needn't reach their ends.
There are 2 independent parts, one for each index of `grp`. The reference program is written for one: setup_inputs(seed, part) draws one part's arguments, and reference() takes and returns one part's arrays. A program takes and returns all parts, laid end to end along the dimension named above; each array names one. Nothing has to cross between parts.
All inputs are finite; a program needn't handle non-finite values.
Results may differ from the reference program's by a relative error of at most 0.0003.
Values sent between devices are 32-bit elements; how exact they have to be, the bound alone decides.
No kernel may reach another device: no remote copies, remote signals or barrier semaphores. Data moves between devices by JAX's collectives and lax.ppermute only.
A program may use at most 64 MiB of HBM per device.

```python
import math
import jax
import jax.numpy as jnp
from jax import lax

JDEV = 1024
NSTARS = 4096
NACT = 6144
N_JA = 4


def touch_ends(result, own_key, smallest, top_value):
    longest = result.shape.index(max(result.shape))
    spots = []
    for shift in (0, 1):
        where = [jax.random.randint(jax.random.fold_in(own_key, axis), (), 0, length) for axis, length in enumerate(result.shape)]
        where[longest] = (where[longest] + shift) % result.shape[longest]
        spots.append(tuple(where))
    return result.at[spots[0]].set(smallest).at[spots[1]].set(top_value)


def level_of(own_key, dims, cuts, low, largest):
    def one(axis_at, shards_of):
        draws = jax.random.uniform(jax.random.fold_in(jax.random.fold_in(own_key, 6), axis_at), (shards_of,), jnp.float32, low / len(cuts), largest / len(cuts))
        return jnp.repeat(jnp.exp(draws), dims[axis_at] // shards_of).reshape((-1,) + (1,) * (len(dims) - axis_at - 1))

    loudness = one(*cuts[0])
    for cut in cuts[1:]:
        loudness = loudness * one(*cut)
    return loudness


def normal_values(key, dims, scale, reach, cuts=(), held_as=jnp.bfloat16):
    values = scale * jax.random.normal(key, dims, jnp.float32)
    if cuts:
        values = values * level_of(key, dims, cuts, -0.22, 0.18)
    return jnp.clip(values, -reach, reach).astype(held_as)


def setup_inputs(seed: int = 0, part: int = 0) -> dict:
    seeds = jax.random.split(jax.random.key(seed), 7)
    part_keys = jax.random.split(jax.random.fold_in(seeds[6], part), 7)
    pos_vel = normal_values(part_keys[0], (6, NSTARS), 1.0, 6.0, ((1, 4),), jnp.float32)
    acc_jerk = normal_values(part_keys[1], (6, NSTARS), 1.0, 6.0, ((1, 4),), jnp.float32)
    mass = jnp.clip(jnp.exp(math.log(0.0007324219) - 2.3025851 * jax.random.uniform(part_keys[2], (NSTARS,), jnp.float32) ** level_of(part_keys[2], (NSTARS,), ((0, 4),), -0.2, 0.2)), 7.324219041038305e-05, 0.0007324219)
    age = jnp.clip(0.125 + 0.375 * jax.random.uniform(part_keys[3], (NSTARS,), jnp.float32) ** level_of(part_keys[3], (NSTARS,), ((0, 4),), -0.2, 0.2), 0.125, 0.5)
    active_local = touch_ends(jax.random.randint(part_keys[4], (NACT,), 0, JDEV), jax.random.fold_in(part_keys[4], 1), 0, JDEV - 1).astype(jnp.int32)
    active_owner = touch_ends(jax.random.randint(part_keys[5], (NACT,), 0, N_JA), jax.random.fold_in(part_keys[5], 1), 0, N_JA - 1).astype(jnp.int32)
    return dict(pos_vel=pos_vel, acc_jerk=acc_jerk, mass=mass, age=age, active_local=active_local, active_owner=active_owner)


soften = 0.0004

def predict(pos_vel, acc_jerk, age):
    position = pos_vel[0:3]
    velocity = pos_vel[3:6]
    accel = acc_jerk[0:3]
    jolt = acc_jerk[3:6]
    step_len = age[None, :]
    new_pos = position + step_len * (velocity + step_len * (accel * 0.5 + step_len * jolt / 6.0))
    new_vel = velocity + step_len * (accel + step_len * jolt * 0.5)
    return jnp.concatenate([new_pos, new_vel], axis=0)

def pair_terms(targets, sources, masses):
    delta_pos = sources[0:3, :, None] - targets[0:3, None, :]
    delta_vel = sources[3:6, :, None] - targets[3:6, None, :]
    dist_sq = lax.optimization_barrier(jnp.sum(delta_pos * delta_pos, axis=0)) + soften
    inverse = lax.rsqrt(dist_sq)
    inv_sq = inverse * inverse
    weighted = masses[:, None] * inverse
    weighted_cube = weighted * inv_sq
    radial = 3.0 * lax.optimization_barrier(jnp.sum(delta_pos * delta_vel, axis=0)) * inv_sq
    accel = lax.optimization_barrier(jnp.sum(weighted_cube[None] * delta_pos, axis=1))
    jolt = lax.optimization_barrier(jnp.sum(weighted_cube[None] * (delta_vel - radial[None] * delta_pos), axis=1))
    potential = -lax.optimization_barrier(jnp.sum(weighted, axis=0))
    return jnp.concatenate([accel, jolt, potential[None]], axis=0)

def correct(history, forces):
    pred_pos = history[0:3]
    pred_vel = history[3:6]
    old_acc = history[6:9]
    old_jolt = history[9:12]
    step_len = history[12:13]
    new_acc = forces[0:3]
    new_jolt = forces[3:6]
    differ = old_acc - new_acc
    square = step_len * step_len
    cubed = square * step_len
    fourth = square * square
    fifth = fourth * step_len
    second = (-6.0 * differ - step_len * (4.0 * old_jolt + 2.0 * new_jolt)) / square
    third = (12.0 * differ + 6.0 * step_len * (old_jolt + new_jolt)) / cubed
    position = pred_pos + fourth / 24.0 * second + fifth / 120.0 * third
    velocity = pred_vel + cubed / 6.0 * second + fourth / 24.0 * third
    return jnp.concatenate([position, velocity], axis=0)

def reference(pos_vel, acc_jerk, mass, age, active_local, active_owner):
    predicted = predict(pos_vel, acc_jerk, age)
    chosen = (active_owner * JDEV + active_local).astype(jnp.int32)
    stacked = jnp.concatenate([predicted, acc_jerk, age[None, :]], axis=0)
    history = jnp.take(stacked, chosen, axis=1)
    targets = history[0:6]
    width = min(512, JDEV)
    nblocks = NSTARS // width
    source_blocks = predicted.reshape(6, nblocks, width).transpose(1, 0, 2)
    mass_blocks = mass.reshape(nblocks, width)

    def accumulate(total, pieces):
        return (total + pair_terms(targets, pieces[0], pieces[1]), None)
    forces, unused = lax.scan(accumulate, jnp.zeros((7, NACT), jnp.float32), (source_blocks, mass_blocks))
    state = correct(history, forces)
    return (state, forces)
```

```python
import jax
import jax.numpy as jnp
from jax import lax
from jax.experimental import pallas as pl
from jax.experimental.pallas import tpu as pltpu
from jax.sharding import PartitionSpec as P

soften = 0.0004
f32 = jnp.float32
bf16 = jnp.bfloat16
LANES = 128
ROWS = 16
COLS = 64
VMEM = pl.BlockSpec(memory_space=pltpu.VMEM)
BOTH_MINOR = (((1,), (1,)), ((), ()))


def predict(pos_vel, acc_jerk, age):
    position = pos_vel[0:3]
    velocity = pos_vel[3:6]
    accel = acc_jerk[0:3]
    jolt = acc_jerk[3:6]
    step_len = age[None, :]
    new_pos = position + step_len * (velocity + step_len * (accel * 0.5 + step_len * jolt / 6.0))
    new_vel = velocity + step_len * (accel + step_len * jolt * 0.5)
    return jnp.concatenate([new_pos, new_vel], axis=0)


def pair_terms(targets, sources, masses):
    delta_pos = sources[0:3, :, None] - targets[0:3, None, :]
    delta_vel = sources[3:6, :, None] - targets[3:6, None, :]
    dist_sq = jnp.sum(delta_pos * delta_pos, axis=0) + soften
    inverse = lax.rsqrt(dist_sq)
    inv_sq = inverse * inverse
    weighted = masses[:, None] * inverse
    weighted_cube = weighted * inv_sq
    radial = 3.0 * jnp.sum(delta_pos * delta_vel, axis=0) * inv_sq
    accel = jnp.sum(weighted_cube[None] * delta_pos, axis=1)
    jolt = jnp.sum(weighted_cube[None] * (delta_vel - radial[None] * delta_pos), axis=1)
    potential = -jnp.sum(weighted, axis=0)
    return jnp.concatenate([accel, jolt, potential[None]], axis=0)


def block_terms(targets, sources, masses):
    count = targets.shape[1]
    width = min(512, count)
    nblocks = count // width
    src_count = sources.shape[1]
    src_width = min(512, src_count)
    src_blocks = src_count // src_width
    source_pieces = sources.reshape(6, src_blocks, src_width).transpose(1, 0, 2)
    mass_pieces = masses.reshape(src_blocks, src_width)
    pieces = targets.reshape(6, nblocks, width).transpose(1, 0, 2)

    def one_block(piece):

        def accumulate(total, parts):
            return (total + pair_terms(piece, parts[0], parts[1]), None)

        total, unused = lax.scan(
            accumulate, jnp.zeros((7, width), jnp.float32), (source_pieces, mass_pieces)
        )
        return total

    results = lax.map(one_block, pieces)
    return results.transpose(1, 0, 2).reshape(7, count)


def correct(pred_pos, pred_vel, old_acc, old_jolt, step_len, new_acc, new_jolt):
    differ = old_acc - new_acc
    square = step_len * step_len
    cubed = square * step_len
    fourth = square * square
    fifth = fourth * step_len
    second = (-6.0 * differ - step_len * (4.0 * old_jolt + 2.0 * new_jolt)) / square
    third = (12.0 * differ + 6.0 * step_len * (old_jolt + new_jolt)) / cubed
    position = pred_pos + fourth / 24.0 * second + fifth / 120.0 * third
    velocity = pred_vel + cubed / 6.0 * second + fourth / 24.0 * third
    return position, velocity


def general(pos_vel, acc_jerk, mass, age, active_local, active_owner):
    shard_rank = lax.axis_index("ja")
    predicted = predict(pos_vel, acc_jerk, age)
    stacked = jnp.concatenate([predicted, acc_jerk, age[None, :]], axis=0)
    picked = jnp.take(stacked, active_local, axis=1)
    owned = active_owner == shard_rank
    contrib = jnp.where(owned[None, :], picked, 0.0)
    history = lax.psum(contrib, "ja")
    partial_value = block_terms(history[0:6], predicted, mass)
    forces = lax.psum(partial_value, "ja")
    position, velocity = correct(
        history[0:3], history[3:6], history[6:9], history[9:12], history[12:13], forces[0:3], forces[3:6]
    )
    return (jnp.concatenate([position, velocity], axis=0), forces)


def predict_kernel(pv_ref, aj_ref, mass_ref, age_ref, src_ref, own_ref):
    width = own_ref.shape[1]
    step_len = age_ref[...]
    accel = aj_ref[0:3, :]
    jolt = aj_ref[3:6, :]
    velocity = pv_ref[3:6, :]
    src_ref[0:3, :] = pv_ref[0:3, :] + step_len * (velocity + step_len * (accel * 0.5 + step_len * jolt / 6.0))
    src_ref[3:6, :] = velocity + step_len * (accel + step_len * jolt * 0.5)
    src_ref[6:7, :] = mass_ref[...]
    src_ref[7:8, :] = step_len
    mine = pl.ds(pl.multiple_of(lax.axis_index("ia") * width, LANES), width)
    own_ref[0:6, :] = src_ref[0:6, mine]
    own_ref[6:12, :] = aj_ref[:, mine]
    own_ref[12:13, :] = age_ref[:, mine]
    own_ref[13:16, :] = jnp.zeros((3, width), f32)


def three_parts(x):
    high = x.astype(bf16).astype(f32)
    rest = x - high
    mid = rest.astype(bf16).astype(f32)
    return high, mid, rest - mid


def spread_targets(own_ref, wide):
    width = own_ref.shape[1]
    turned = jnp.transpose(own_ref[0:8, :])
    for c in range(6):
        wide[c] = jnp.broadcast_to(turned[:, c : c + 1], (width, LANES))


def clear_features(feat):
    count = feat.shape[2]
    feat[...] = jnp.zeros(feat.shape, f32)
    one = jnp.ones((1, count), f32)
    feat[0, 18:19, :] = one
    feat[1, 41:42, :] = one


def source_features(source, feat, right, width):
    rows = 0
    for x in (*three_parts(source[0:3, :]), *three_parts(source[3:6, :])):
        feat[0, rows : rows + 3, :] = x
        if rows < 9:
            feat[1, 32 + rows : 35 + rows, :] = x
        rows += 3
    for k in range(right.shape[0]):
        for i in range(4):
            right[k, :, i * width : i * width + width] = feat[i // 2, :, k * width : k * width + width].astype(bf16)


def pair_chunk(source, offset, wide, left, pot_ref, diagonal):
    width = wide.shape[1]
    for rb in range(width // ROWS):
        rs = slice(rb * ROWS, rb * ROWS + ROWS)
        target = [wide[c, rs, :] for c in range(6)]
        pot = pot_ref[rs, :]
        for j in range(width // LANES):
            cs = pl.ds(offset + LANES * j, LANES)
            row = [jnp.broadcast_to(source[c : c + 1, cs], (ROWS, LANES)) for c in range(7)]
            dx, dy, dz = (row[c] - target[c] for c in range(3))
            ex, ey, ez = (row[c] - target[c] for c in range(3, 6))
            inverse = lax.rsqrt(((dx * dx + soften) + dy * dy) + dz * dz)
            inv_sq = inverse * inverse
            weighted = row[6] * inverse
            pot = pot + weighted
            cube = weighted * inv_sq
            if diagonal and rb * ROWS // LANES == j:
                here = lax.broadcasted_iota(jnp.int32, (ROWS, LANES), 0) + (rb * ROWS - j * LANES)
                there = lax.broadcasted_iota(jnp.int32, (ROWS, LANES), 1)
                cube = jnp.where(here == there, 0.0, cube)
            radial = cube * ((dx * ex + dy * ey + dz * ez) * inv_sq)
            parts = (
                cube,
                cube - cube.astype(bf16).astype(f32),
                radial,
                radial - radial.astype(bf16).astype(f32),
            )
            for i, x in enumerate(parts):
                left[rs, i * width + LANES * j : i * width + LANES * j + LANES] = x
        pot_ref[rs, :] = pot


def add_chunk(left, right, sum_ref):
    sum_ref[...] += lax.dot_general(left[...].astype(bf16), right, BOTH_MINOR, preferred_element_type=f32)


def local_kernel(src_ref, own_ref, sum_ref, pot_ref, feat, right, wide, left):
    width = own_ref.shape[1]
    chunks = right.shape[0]
    spread_targets(own_ref, wide)
    clear_features(feat)
    source_features(src_ref, feat, right, width)
    sum_ref[...] = jnp.zeros(sum_ref.shape, f32)
    pot_ref[...] = jnp.zeros(pot_ref.shape, f32)
    first = lax.axis_index("ia")
    turn = [lax.rem(first + k, chunks) for k in range(chunks)]
    for k in range(chunks):
        pair_chunk(src_ref, pl.multiple_of(turn[k] * width, LANES), wide, left.at[k % 2], pot_ref, k == 0)
        if k:
            add_chunk(left.at[(k - 1) % 2], right[turn[k - 1]], sum_ref)
    add_chunk(left.at[(chunks - 1) % 2], right[turn[chunks - 1]], sum_ref)


def remote_kernel(*refs):
    count = len(refs) - 8
    sources = refs[:count]
    own_ref, sum_in, pot_in, out_ref, feat, right, wide, left = refs[count:]
    pl.run_scoped(
        lambda sum_ref, pot_ref: remote_body(
            sources, own_ref, sum_in, pot_in, out_ref, feat, right, wide, left, sum_ref, pot_ref
        ),
        pltpu.VMEM(sum_in.shape, f32),
        pltpu.VMEM(pot_in.shape, f32),
    )


def remote_body(sources, own_ref, sum_in, pot_in, out_ref, feat, right, wide, left, sum_ref, pot_ref):
    width = own_ref.shape[1]
    chunks = right.shape[0]
    spread_targets(own_ref, wide)
    clear_features(feat)
    sum_ref[...] = sum_in[...]
    pot_ref[...] = pot_in[...]
    for source in sources:
        source_features(source, feat, right, width)
        pair_chunk(source, 0, wide, left.at[0], pot_ref, False)

        def two(i, unused):
            pair_chunk(source, pl.multiple_of((2 * i + 1) * width, LANES), wide, left.at[1], pot_ref, False)
            add_chunk(left.at[0], right[2 * i], sum_ref)
            pair_chunk(source, pl.multiple_of((2 * i + 2) * width, LANES), wide, left.at[0], pot_ref, False)
            add_chunk(left.at[1], right[2 * i + 1], sum_ref)
            return 0

        lax.fori_loop(0, (chunks - 2) // 2, two, 0)
        pair_chunk(source, (chunks - 1) * width, wide, left.at[1], pot_ref, False)
        add_chunk(left.at[0], right[chunks - 2], sum_ref)
        add_chunk(left.at[1], right[chunks - 1], sum_ref)
    sums = jnp.transpose(sum_ref[...])
    pot = jnp.sum(jnp.transpose(pot_ref[...]), axis=0, keepdims=True)
    pos = own_ref[0:3, :]
    vel = own_ref[3:6, :]
    total = sums[18:19, :]
    new_acc = (sums[0:3, :] - pos * total) + sums[3:6, :] + sums[6:9, :]
    flow = (sums[9:12, :] - vel * total) + sums[12:15, :] + sums[15:18, :]
    pull = (sums[32:35, :] - pos * sums[41:42, :]) + sums[35:38, :] + sums[38:41, :]
    new_jolt = flow - 3.0 * pull
    position, velocity = correct(
        pos, vel, own_ref[6:9, :], own_ref[9:12, :], own_ref[12:13, :], new_acc, new_jolt
    )
    out_ref[0:3, :] = position
    out_ref[3:6, :] = velocity
    out_ref[6:8, :] = jnp.zeros((2, width), f32)
    out_ref[8:11, :] = new_acc
    out_ref[11:14, :] = new_jolt
    out_ref[14:15, :] = -pot
    out_ref[15:16, :] = jnp.zeros((1, width), f32)


def pick_kernel(ia_bits, ja_bits, width, table_ref, local_ref, owner_ref, state_ref, forces_ref):
    count = local_ref.shape[1]
    per = width // LANES
    my_ja = lax.axis_index("ja")
    my_ia = lax.axis_index("ia")
    for b in range(count // LANES):
        cs = slice(b * LANES, b * LANES + LANES)
        local = local_ref[:, cs]
        apart_ja = lax.bitwise_xor(owner_ref[:, cs], my_ja)
        apart_ia = lax.bitwise_xor(local // width, my_ia)
        parity = apart_ia
        for i in range(1, ia_bits):
            parity = lax.bitwise_xor(parity, lax.shift_right_logical(apart_ia, i))
        flips = parity
        for i in range(ja_bits):
            flips = lax.bitwise_xor(flips, lax.shift_right_logical(apart_ja, i))
        slot = apart_ja + lax.shift_left(lax.shift_right_logical(apart_ia, 1), ja_bits)
        slot = slot + lax.shift_left(lax.bitwise_and(flips, 1), ja_bits + ia_bits - 1)
        within = lax.rem(local, width)
        piece = jnp.broadcast_to(slot * per + within // LANES, (8, LANES))
        lane = jnp.broadcast_to(lax.rem(within, LANES), (8, LANES))
        state = jnp.zeros((8, LANES), f32)
        forces = jnp.zeros((8, LANES), f32)
        for t in range(table_ref.shape[1] // LANES):
            hit = piece == t
            ts = slice(t * LANES, t * LANES + LANES)
            state = jnp.where(hit, jnp.take_along_axis(table_ref[0:8, ts], lane, axis=1), state)
            forces = jnp.where(hit, jnp.take_along_axis(table_ref[8:16, ts], lane, axis=1), forces)
        state_ref[:, cs] = state[0:6, :]
        forces_ref[:, cs] = forces[0:7, :]


def shape_of(*dims):
    return jax.ShapeDtypeStruct(dims, f32)


def all_stars(nj, ni, pos_vel, acc_jerk, mass, age, active_local, active_owner):
    stars = mass.shape[0]
    width = stars // ni
    chunks = stars // width
    ja_bits = nj.bit_length() - 1
    ia_bits = ni.bit_length() - 1

    def exchange(x, dj, di):
        pairs = [(j * ni + i, (j ^ dj) * ni + (i ^ di)) for j in range(nj) for i in range(ni)]
        return lax.ppermute(x, ("ja", "ia"), pairs)

    src, own = pl.pallas_call(
        predict_kernel,
        out_shape=(shape_of(8, stars), shape_of(16, width)),
        in_specs=[VMEM] * 4,
        out_specs=(VMEM, VMEM),
        name="predict",
    )(pos_vel, acc_jerk, mass[None, :], age[None, :])
    others = [exchange(src, d, 1) for d in range(1, nj)]
    scratch = [
        pltpu.VMEM((2, COLS, stars), f32),
        pltpu.VMEM((chunks, COLS, 4 * width), bf16),
        pltpu.VMEM((6, width, LANES), f32),
        pltpu.VMEM((2, width, 4 * width), f32),
    ]
    pairs_cost = pl.CostEstimate(flops=40 * width * stars, transcendentals=width * stars, bytes_accessed=400000)
    sums, pot = pl.pallas_call(
        local_kernel,
        out_shape=(shape_of(width, COLS), shape_of(width, LANES)),
        in_specs=[VMEM] * 2,
        out_specs=(VMEM, VMEM),
        scratch_shapes=scratch,
        cost_estimate=pairs_cost,
        name="near",
    )(src, own)
    block = pl.pallas_call(
        remote_kernel,
        out_shape=shape_of(16, width),
        in_specs=[VMEM] * (len(others) + 3),
        out_specs=VMEM,
        scratch_shapes=scratch,
        name="far",
    )(*others, own, sums, pot)
    for bit in range(ja_bits):
        block = jnp.concatenate([block, exchange(block, 1 << bit, 1)], axis=1)
    for bit in range(1, ia_bits):
        block = jnp.concatenate([block, exchange(block, 0, (1 << bit) + 1)], axis=1)
    block = jnp.concatenate([block, exchange(block, 0, 1)], axis=1)
    count = active_local.shape[0]

    def pick(*refs):
        pick_kernel(ia_bits, ja_bits, width, *refs)

    return pl.pallas_call(
        pick,
        out_shape=(shape_of(6, count), shape_of(7, count)),
        in_specs=[VMEM] * 3,
        out_specs=(VMEM, VMEM),
        name="pick",
    )(block, active_local[None, :], active_owner[None, :])


def solution(mesh):
    nj = mesh.shape["ja"]
    ni = mesh.shape["ia"]

    def local(pos_vel, acc_jerk, mass, age, active_local, active_owner):
        stars = mass.shape[0]
        width = stars // ni
        fits = (
            nj & (nj - 1) == 0
            and ni & (ni - 1) == 0
            and nj > 1
            and ni > 1
            and stars % ni == 0
            and width % LANES == 0
            and width <= 256
            and active_local.shape[0] % LANES == 0
            and stars * nj <= active_local.shape[0] * ni
        )
        args = (pos_vel, acc_jerk, mass, age, active_local, active_owner)
        return all_stars(nj, ni, *args) if fits else general(*args)

    return jax.shard_map(
        local,
        mesh=mesh,
        in_specs=(
            P(None, ("grp", "ja")),
            P(None, ("grp", "ja")),
            P(("grp", "ja")),
            P(("grp", "ja")),
            P(("grp", "ia")),
            P(("grp", "ia")),
        ),
        out_specs=(P(None, ("grp", "ia")), P(None, ("grp", "ia"))),
        check_vma=False,
    )
```

```python
import jax
import jax.numpy as jnp
from jax import lax
from jax.experimental import pallas as pl
from jax.experimental.pallas import tpu as pltpu
from jax.sharding import PartitionSpec as P

soften = 0.0004
f32 = jnp.float32
bf16 = jnp.bfloat16
LANES = 128
ROWS = 16
COLS = 64
VMEM = pl.BlockSpec(memory_space=pltpu.VMEM)
PARAMS = pltpu.CompilerParams(vmem_limit_bytes=16 << 20)
BOTH_MINOR = (((1,), (1,)), ((), ()))


def predict(pos_vel, acc_jerk, age):
    position = pos_vel[0:3]
    velocity = pos_vel[3:6]
    accel = acc_jerk[0:3]
    jolt = acc_jerk[3:6]
    step_len = age[None, :]
    new_pos = position + step_len * (velocity + step_len * (accel * 0.5 + step_len * jolt / 6.0))
    new_vel = velocity + step_len * (accel + step_len * jolt * 0.5)
    return jnp.concatenate([new_pos, new_vel], axis=0)


def pair_terms(targets, sources, masses):
    delta_pos = sources[0:3, :, None] - targets[0:3, None, :]
    delta_vel = sources[3:6, :, None] - targets[3:6, None, :]
    dist_sq = jnp.sum(delta_pos * delta_pos, axis=0) + soften
    inverse = lax.rsqrt(dist_sq)
    inv_sq = inverse * inverse
    weighted = masses[:, None] * inverse
    weighted_cube = weighted * inv_sq
    radial = 3.0 * jnp.sum(delta_pos * delta_vel, axis=0) * inv_sq
    accel = jnp.sum(weighted_cube[None] * delta_pos, axis=1)
    jolt = jnp.sum(weighted_cube[None] * (delta_vel - radial[None] * delta_pos), axis=1)
    potential = -jnp.sum(weighted, axis=0)
    return jnp.concatenate([accel, jolt, potential[None]], axis=0)


def block_terms(targets, sources, masses):
    count = targets.shape[1]
    width = min(512, count)
    nblocks = count // width
    src_count = sources.shape[1]
    src_width = min(512, src_count)
    src_blocks = src_count // src_width
    source_pieces = sources.reshape(6, src_blocks, src_width).transpose(1, 0, 2)
    mass_pieces = masses.reshape(src_blocks, src_width)
    pieces = targets.reshape(6, nblocks, width).transpose(1, 0, 2)

    def one_block(piece):

        def accumulate(total, parts):
            return (total + pair_terms(piece, parts[0], parts[1]), None)

        total, unused = lax.scan(
            accumulate, jnp.zeros((7, width), jnp.float32), (source_pieces, mass_pieces)
        )
        return total

    results = lax.map(one_block, pieces)
    return results.transpose(1, 0, 2).reshape(7, count)


def correct(pred_pos, pred_vel, old_acc, old_jolt, step_len, new_acc, new_jolt):
    differ = old_acc - new_acc
    square = step_len * step_len
    cubed = square * step_len
    fourth = square * square
    fifth = fourth * step_len
    second = (-6.0 * differ - step_len * (4.0 * old_jolt + 2.0 * new_jolt)) / square
    third = (12.0 * differ + 6.0 * step_len * (old_jolt + new_jolt)) / cubed
    position = pred_pos + fourth / 24.0 * second + fifth / 120.0 * third
    velocity = pred_vel + cubed / 6.0 * second + fourth / 24.0 * third
    return position, velocity


def general(pos_vel, acc_jerk, mass, age, active_local, active_owner):
    shard_rank = lax.axis_index("ja")
    predicted = predict(pos_vel, acc_jerk, age)
    stacked = jnp.concatenate([predicted, acc_jerk, age[None, :]], axis=0)
    picked = jnp.take(stacked, active_local, axis=1)
    owned = active_owner == shard_rank
    contrib = jnp.where(owned[None, :], picked, 0.0)
    history = lax.psum(contrib, "ja")
    partial_value = block_terms(history[0:6], predicted, mass)
    forces = lax.psum(partial_value, "ja")
    position, velocity = correct(
        history[0:3], history[3:6], history[6:9], history[9:12], history[12:13], forces[0:3], forces[3:6]
    )
    return (jnp.concatenate([position, velocity], axis=0), forces)


def predict_kernel(pv_hbm, aj_hbm, mass_hbm, age_hbm, src_ref, own_ref, pv_ref, aj_ref, mass_ref, age_ref, sems):
    copies = [
        pltpu.make_async_copy(hbm, ref, sems.at[i])
        for i, (hbm, ref) in enumerate(
            ((pv_hbm, pv_ref), (aj_hbm, aj_ref), (mass_hbm, mass_ref), (age_hbm, age_ref))
        )
    ]
    for copy in copies:
        copy.start()
    for copy in copies:
        copy.wait()
    width = own_ref.shape[1]
    step_len = age_ref[...]
    accel = aj_ref[0:3, :]
    jolt = aj_ref[3:6, :]
    velocity = pv_ref[3:6, :]
    src_ref[0:3, :] = pv_ref[0:3, :] + step_len * (velocity + step_len * (accel * 0.5 + step_len * jolt / 6.0))
    src_ref[3:6, :] = velocity + step_len * (accel + step_len * jolt * 0.5)
    src_ref[6:7, :] = mass_ref[...]
    src_ref[7:8, :] = step_len
    mine = pl.ds(pl.multiple_of(lax.axis_index("ia") * width, LANES), width)
    own_ref[0:6, :] = src_ref[0:6, mine]
    own_ref[6:12, :] = aj_ref[:, mine]
    own_ref[12:13, :] = age_ref[:, mine]
    own_ref[13:16, :] = jnp.zeros((3, width), f32)


def three_parts(x):
    high = x.astype(bf16).astype(f32)
    rest = x - high
    mid = rest.astype(bf16).astype(f32)
    return high, mid, rest - mid


def spread_targets(own_ref, wide):
    width = own_ref.shape[1]
    turned = jnp.transpose(own_ref[0:8, :])
    for c in range(6):
        wide[c] = jnp.broadcast_to(turned[:, c : c + 1], (width, LANES))


def clear_features(feat):
    count = feat.shape[2]
    feat[...] = jnp.zeros(feat.shape, f32)
    one = jnp.ones((1, count), f32)
    feat[0, 18:19, :] = one
    feat[1, 41:42, :] = one


def source_features(source, feat, right, width):
    rows = 0
    for x in (*three_parts(source[0:3, :]), *three_parts(source[3:6, :])):
        feat[0, rows : rows + 3, :] = x
        if rows < 9:
            feat[1, 32 + rows : 35 + rows, :] = x
        rows += 3
    for k in range(right.shape[0]):
        for i in range(4):
            right[k, :, i * width : i * width + width] = feat[i // 2, :, k * width : k * width + width].astype(bf16)


def pair_chunk(source, offset, wide, left, pot_ref, diagonal):
    width = wide.shape[1]
    for rb in range(width // ROWS):
        rs = slice(rb * ROWS, rb * ROWS + ROWS)
        target = [wide[c, rs, :] for c in range(6)]
        pot = pot_ref[rs, :]
        for j in range(width // LANES):
            cs = pl.ds(offset + LANES * j, LANES)
            row = [jnp.broadcast_to(source[c : c + 1, cs], (ROWS, LANES)) for c in range(7)]
            dx, dy, dz = (row[c] - target[c] for c in range(3))
            ex, ey, ez = (row[c] - target[c] for c in range(3, 6))
            inverse = lax.rsqrt(((dx * dx + soften) + dy * dy) + dz * dz)
            inv_sq = inverse * inverse
            weighted = row[6] * inverse
            pot = pot + weighted
            cube = weighted * inv_sq
            if diagonal and rb * ROWS // LANES == j:
                here = lax.broadcasted_iota(jnp.int32, (ROWS, LANES), 0) + (rb * ROWS - j * LANES)
                there = lax.broadcasted_iota(jnp.int32, (ROWS, LANES), 1)
                cube = jnp.where(here == there, 0.0, cube)
            radial = cube * ((dx * ex + dy * ey + dz * ez) * inv_sq)
            parts = (
                cube,
                cube - cube.astype(bf16).astype(f32),
                radial,
                radial - radial.astype(bf16).astype(f32),
            )
            for i, x in enumerate(parts):
                left[rs, i * width + LANES * j : i * width + LANES * j + LANES] = x
        pot_ref[rs, :] = pot


def add_chunk(left, right, sum_ref):
    sum_ref[...] += lax.dot_general(left[...].astype(bf16), right, BOTH_MINOR, preferred_element_type=f32)


def local_kernel(src_ref, own_ref, sum_ref, pot_ref, feat, right, wide, left):
    width = own_ref.shape[1]
    chunks = right.shape[0]
    spread_targets(own_ref, wide)
    clear_features(feat)
    source_features(src_ref, feat, right, width)
    sum_ref[...] = jnp.zeros(sum_ref.shape, f32)
    pot_ref[...] = jnp.zeros(pot_ref.shape, f32)
    first = lax.axis_index("ia")
    turn = [lax.rem(first + k, chunks) for k in range(chunks)]
    for k in range(chunks):
        pair_chunk(src_ref, pl.multiple_of(turn[k] * width, LANES), wide, left.at[k % 2], pot_ref, k == 0)
        if k:
            add_chunk(left.at[(k - 1) % 2], right[turn[k - 1]], sum_ref)
    add_chunk(left.at[(chunks - 1) % 2], right[turn[chunks - 1]], sum_ref)


def remote_kernel(*refs):
    count = len(refs) - 8
    sources = refs[:count]
    own_ref, sum_in, pot_in, out_ref, feat, right, wide, left = refs[count:]
    pl.run_scoped(
        lambda sum_ref, pot_ref: remote_body(
            sources, own_ref, sum_in, pot_in, out_ref, feat, right, wide, left, sum_ref, pot_ref
        ),
        pltpu.VMEM(sum_in.shape, f32),
        pltpu.VMEM(pot_in.shape, f32),
    )


def remote_body(sources, own_ref, sum_in, pot_in, out_ref, feat, right, wide, left, sum_ref, pot_ref):
    width = own_ref.shape[1]
    chunks = right.shape[0]
    spread_targets(own_ref, wide)
    clear_features(feat)
    sum_ref[...] = sum_in[...]
    pot_ref[...] = pot_in[...]
    for source in sources:
        source_features(source, feat, right, width)
        pair_chunk(source, 0, wide, left.at[0], pot_ref, False)

        def two(i, unused):
            pair_chunk(source, pl.multiple_of((2 * i + 1) * width, LANES), wide, left.at[1], pot_ref, False)
            add_chunk(left.at[0], right[2 * i], sum_ref)
            pair_chunk(source, pl.multiple_of((2 * i + 2) * width, LANES), wide, left.at[0], pot_ref, False)
            add_chunk(left.at[1], right[2 * i + 1], sum_ref)
            return 0

        lax.fori_loop(0, (chunks - 2) // 2, two, 0)
        pair_chunk(source, (chunks - 1) * width, wide, left.at[1], pot_ref, False)
        add_chunk(left.at[0], right[chunks - 2], sum_ref)
        add_chunk(left.at[1], right[chunks - 1], sum_ref)
    sums = jnp.transpose(sum_ref[...])
    pot = jnp.sum(jnp.transpose(pot_ref[...]), axis=0, keepdims=True)
    pos = own_ref[0:3, :]
    vel = own_ref[3:6, :]
    total = sums[18:19, :]
    new_acc = (sums[0:3, :] - pos * total) + sums[3:6, :] + sums[6:9, :]
    flow = (sums[9:12, :] - vel * total) + sums[12:15, :] + sums[15:18, :]
    pull = (sums[32:35, :] - pos * sums[41:42, :]) + sums[35:38, :] + sums[38:41, :]
    new_jolt = flow - 3.0 * pull
    position, velocity = correct(
        pos, vel, own_ref[6:9, :], own_ref[9:12, :], own_ref[12:13, :], new_acc, new_jolt
    )
    out_ref[0:3, :] = position
    out_ref[3:6, :] = velocity
    out_ref[6:8, :] = jnp.zeros((2, width), f32)
    out_ref[8:11, :] = new_acc
    out_ref[11:14, :] = new_jolt
    out_ref[14:15, :] = -pot
    out_ref[15:16, :] = jnp.zeros((1, width), f32)


def pick_kernel(ia_bits, ja_bits, width, first_slot, last, refs):
    table_ref, local_ref, owner_ref = refs[:3]
    before = refs[3:-2]
    state_ref, forces_ref = refs[-2:]
    count = local_ref.shape[0]
    per = width // LANES
    my_ja = lax.axis_index("ja")
    my_ia = lax.axis_index("ia")
    for b in range(count // LANES):
        cs = slice(b * LANES, b * LANES + LANES)
        local = local_ref[cs].reshape(1, LANES)
        apart_ja = lax.bitwise_xor(owner_ref[cs].reshape(1, LANES), my_ja)
        apart_ia = lax.bitwise_xor(local // width, my_ia)
        flips = apart_ia + (apart_ja != 0).astype(jnp.int32)
        for i in range(1, ia_bits):
            flips = flips + lax.shift_right_logical(apart_ia, i)
        slot = apart_ja + lax.shift_left(lax.shift_right_logical(apart_ia, 1), ja_bits)
        slot = slot + lax.shift_left(lax.bitwise_and(flips, 1), ja_bits + ia_bits - 1)
        within = lax.rem(local, width)
        piece = jnp.broadcast_to((slot - first_slot) * per + within // LANES, (8, LANES))
        lane = jnp.broadcast_to(lax.rem(within, LANES), (8, LANES))
        state = before[0][:, cs] if before else jnp.zeros((8, LANES), f32)
        forces = before[1][:, cs] if before else jnp.zeros((8, LANES), f32)
        for t in range(table_ref.shape[1] // LANES):
            hit = piece == t
            ts = slice(t * LANES, t * LANES + LANES)
            state = jnp.where(hit, jnp.take_along_axis(table_ref[0:8, ts], lane, axis=1), state)
            forces = jnp.where(hit, jnp.take_along_axis(table_ref[8:16, ts], lane, axis=1), forces)
        state_ref[:, cs] = state[0 : state_ref.shape[0], :]
        forces_ref[:, cs] = forces[0 : forces_ref.shape[0], :]


def shape_of(*dims):
    return jax.ShapeDtypeStruct(dims, f32)


def all_stars(nj, ni, pos_vel, acc_jerk, mass, age, active_local, active_owner):
    stars = mass.shape[0]
    width = stars // ni
    chunks = stars // width
    ja_bits = nj.bit_length() - 1
    ia_bits = ni.bit_length() - 1

    def exchange(x, dj, di):
        pairs = [(j * ni + i, (j ^ dj) * ni + (i ^ di)) for j in range(nj) for i in range(ni)]
        return lax.ppermute(x, ("ja", "ia"), pairs)

    src, own = pl.pallas_call(
        predict_kernel,
        out_shape=(shape_of(8, stars), shape_of(16, width)),
        in_specs=[pl.BlockSpec(memory_space=pltpu.HBM)] * 4,
        out_specs=(VMEM, VMEM),
        scratch_shapes=[
            pltpu.VMEM((6, stars), f32),
            pltpu.VMEM((6, stars), f32),
            pltpu.VMEM((1, stars), f32),
            pltpu.VMEM((1, stars), f32),
            pltpu.SemaphoreType.DMA((4,)),
        ],
        compiler_params=PARAMS,
        name="predict",
    )(*(pltpu.with_memory_space_constraint(x, pltpu.HBM) for x in (pos_vel, acc_jerk, mass[None, :], age[None, :])))
    others = [exchange(src, d, 1) for d in range(1, nj)]
    scratch = [
        pltpu.VMEM((2, COLS, stars), f32),
        pltpu.VMEM((chunks, COLS, 4 * width), bf16),
        pltpu.VMEM((6, width, LANES), f32),
        pltpu.VMEM((2, width, 4 * width), f32),
    ]
    pairs_cost = pl.CostEstimate(flops=40 * width * stars, transcendentals=width * stars, bytes_accessed=400000)
    sums, pot = pl.pallas_call(
        local_kernel,
        out_shape=(shape_of(width, COLS), shape_of(width, LANES)),
        in_specs=[VMEM] * 2,
        out_specs=(VMEM, VMEM),
        scratch_shapes=scratch,
        cost_estimate=pairs_cost,
        compiler_params=PARAMS,
        name="near",
    )(src, own)
    block = pl.pallas_call(
        remote_kernel,
        out_shape=shape_of(16, width),
        in_specs=[VMEM] * (len(others) + 3),
        out_specs=VMEM,
        scratch_shapes=scratch,
        compiler_params=PARAMS,
        name="far",
    )(*others, own, sums, pot)
    count = active_local.shape[0]

    def pick(table, first_slot, before, last=False):
        return pl.pallas_call(
            lambda *refs: pick_kernel(ia_bits, ja_bits, width, first_slot, last, refs),
            out_shape=(shape_of(6 if last else 8, count), shape_of(7 if last else 8, count)),
            in_specs=[VMEM] * (3 + len(before)),
            out_specs=(VMEM, VMEM),
            compiler_params=PARAMS,
            cost_estimate=pl.CostEstimate(flops=count * table.shape[1], transcendentals=0, bytes_accessed=400000),
            name="pick",
        )(table, active_local, active_owner, *before)

    table = jnp.concatenate([block, *(exchange(block, d, 1) for d in range(1, nj))], axis=1)
    slots = nj
    fresh, first_slot, found = table, 0, ()
    for step in [(1 << bit) + 1 for bit in range(1, ia_bits)] + [1]:
        came = exchange(table, 0, step)
        found = pick(fresh, first_slot, found)
        fresh, first_slot = came, slots
        if step != 1:
            table = jnp.concatenate([table, came], axis=1)
        slots *= 2
    return tuple(pick(fresh, first_slot, found, True))


def solution(mesh):
    nj = mesh.shape["ja"]
    ni = mesh.shape["ia"]

    def local(pos_vel, acc_jerk, mass, age, active_local, active_owner):
        stars = mass.shape[0]
        width = stars // ni
        fits = (
            nj & (nj - 1) == 0
            and ni & (ni - 1) == 0
            and 1 < nj <= 8
            and ni > 1
            and stars % ni == 0
            and width % LANES == 0
            and width <= 256
            and active_local.shape[0] % LANES == 0
            and stars * nj <= active_local.shape[0] * ni
        )
        args = (pos_vel, acc_jerk, mass, age, active_local, active_owner)
        return all_stars(nj, ni, *args) if fits else general(*args)

    return jax.shard_map(
        local,
        mesh=mesh,
        in_specs=(
            P(None, ("grp", "ja")),
            P(None, ("grp", "ja")),
            P(("grp", "ja")),
            P(("grp", "ja")),
            P(("grp", "ia")),
            P(("grp", "ia")),
        ),
        out_specs=(P(None, ("grp", "ia")), P(None, ("grp", "ia"))),
        check_vma=False,
    )
```

```python
import jax
import jax.numpy as jnp
from jax import lax
from jax.experimental import pallas as pl
from jax.experimental.pallas import tpu as pltpu
from jax.sharding import PartitionSpec as P

soften = 0.0004
f32 = jnp.float32
bf16 = jnp.bfloat16
LANES = 128
ROWS = 16
COLS = 64
VMEM = pl.BlockSpec(memory_space=pltpu.VMEM)
PARAMS = pltpu.CompilerParams(vmem_limit_bytes=16 << 20)
BOTH_MINOR = (((1,), (1,)), ((), ()))


def predict(pos_vel, acc_jerk, age):
    position = pos_vel[0:3]
    velocity = pos_vel[3:6]
    accel = acc_jerk[0:3]
    jolt = acc_jerk[3:6]
    step_len = age[None, :]
    new_pos = position + step_len * (velocity + step_len * (accel * 0.5 + step_len * jolt / 6.0))
    new_vel = velocity + step_len * (accel + step_len * jolt * 0.5)
    return jnp.concatenate([new_pos, new_vel], axis=0)


def pair_terms(targets, sources, masses):
    delta_pos = sources[0:3, :, None] - targets[0:3, None, :]
    delta_vel = sources[3:6, :, None] - targets[3:6, None, :]
    dist_sq = jnp.sum(delta_pos * delta_pos, axis=0) + soften
    inverse = lax.rsqrt(dist_sq)
    inv_sq = inverse * inverse
    weighted = masses[:, None] * inverse
    weighted_cube = weighted * inv_sq
    radial = 3.0 * jnp.sum(delta_pos * delta_vel, axis=0) * inv_sq
    accel = jnp.sum(weighted_cube[None] * delta_pos, axis=1)
    jolt = jnp.sum(weighted_cube[None] * (delta_vel - radial[None] * delta_pos), axis=1)
    potential = -jnp.sum(weighted, axis=0)
    return jnp.concatenate([accel, jolt, potential[None]], axis=0)


def block_terms(targets, sources, masses):
    count = targets.shape[1]
    width = min(512, count)
    nblocks = count // width
    src_count = sources.shape[1]
    src_width = min(512, src_count)
    src_blocks = src_count // src_width
    source_pieces = sources.reshape(6, src_blocks, src_width).transpose(1, 0, 2)
    mass_pieces = masses.reshape(src_blocks, src_width)
    pieces = targets.reshape(6, nblocks, width).transpose(1, 0, 2)

    def one_block(piece):

        def accumulate(total, parts):
            return (total + pair_terms(piece, parts[0], parts[1]), None)

        total, unused = lax.scan(
            accumulate, jnp.zeros((7, width), jnp.float32), (source_pieces, mass_pieces)
        )
        return total

    results = lax.map(one_block, pieces)
    return results.transpose(1, 0, 2).reshape(7, count)


def correct(pred_pos, pred_vel, old_acc, old_jolt, step_len, new_acc, new_jolt):
    differ = old_acc - new_acc
    square = step_len * step_len
    cubed = square * step_len
    fourth = square * square
    fifth = fourth * step_len
    second = (-6.0 * differ - step_len * (4.0 * old_jolt + 2.0 * new_jolt)) / square
    third = (12.0 * differ + 6.0 * step_len * (old_jolt + new_jolt)) / cubed
    position = pred_pos + fourth / 24.0 * second + fifth / 120.0 * third
    velocity = pred_vel + cubed / 6.0 * second + fourth / 24.0 * third
    return position, velocity


def general(pos_vel, acc_jerk, mass, age, active_local, active_owner):
    shard_rank = lax.axis_index("ja")
    predicted = predict(pos_vel, acc_jerk, age)
    stacked = jnp.concatenate([predicted, acc_jerk, age[None, :]], axis=0)
    picked = jnp.take(stacked, active_local, axis=1)
    owned = active_owner == shard_rank
    contrib = jnp.where(owned[None, :], picked, 0.0)
    history = lax.psum(contrib, "ja")
    partial_value = block_terms(history[0:6], predicted, mass)
    forces = lax.psum(partial_value, "ja")
    position, velocity = correct(
        history[0:3], history[3:6], history[6:9], history[9:12], history[12:13], forces[0:3], forces[3:6]
    )
    return (jnp.concatenate([position, velocity], axis=0), forces)


def predict_kernel(pv_hbm, aj_hbm, mass_hbm, age_hbm, src_ref, long_ref, own_ref, mid_ref, pv_ref, aj_ref, mass_ref, age_ref, sems):
    copies = [
        pltpu.make_async_copy(hbm, ref, sems.at[i])
        for i, (hbm, ref) in enumerate(
            ((pv_hbm, pv_ref), (aj_hbm, aj_ref), (mass_hbm, mass_ref), (age_hbm, age_ref))
        )
    ]
    for copy in copies:
        copy.start()
    for copy in copies:
        copy.wait()
    width = own_ref.shape[1]
    stars = src_ref.shape[1]
    step_len = age_ref[...]
    accel = aj_ref[0:3, :]
    jolt = aj_ref[3:6, :]
    velocity = pv_ref[3:6, :]
    src_ref[0:3, :] = pv_ref[0:3, :] + step_len * (velocity + step_len * (accel * 0.5 + step_len * jolt / 6.0))
    src_ref[3:6, :] = velocity + step_len * (accel + step_len * jolt * 0.5)
    src_ref[6:7, :] = mass_ref[...]
    src_ref[7:8, :] = step_len
    long_ref[:, 0:stars] = src_ref[...]
    rank = lax.axis_index("ia")
    mine = pl.ds(pl.multiple_of(rank * width, LANES), width)
    partner = pl.ds(pl.multiple_of(lax.bitwise_xor(rank, 1) * width, LANES), width)
    long_ref[0:6, stars : stars + width] = aj_ref[:, partner]
    long_ref[6:8, stars : stars + width] = jnp.zeros((2, width), f32)
    own_ref[0:8, :] = src_ref[:, mine]
    own_ref[8:14, :] = aj_ref[:, mine]
    own_ref[14:16, :] = jnp.zeros((2, width), f32)
    mean = jnp.sum(src_ref[:, mine], axis=1, keepdims=True) * (1.0 / width)
    mid_ref[...] = jnp.broadcast_to(mean, (8, LANES))


def three_parts(x):
    high = x.astype(bf16).astype(f32)
    rest = x - high
    mid = rest.astype(bf16).astype(f32)
    return high, mid, rest - mid


def centred(rows, mid_ref):
    middle = jnp.concatenate([mid_ref[...]] * (rows.shape[1] // LANES), axis=1)
    return rows[0:3, :] - middle[0:3, :], rows[3:6, :] - middle[3:6, :]


def dot_parts(a, b):
    return three_parts(jnp.sum(a * b, axis=0, keepdims=True))


def set_targets(own_ref, mid_ref, wide, near_feat, rows_ref):
    width = own_ref.shape[1]
    turned = jnp.transpose(own_ref[0:8, :])
    for c in range(3):
        wide[c] = jnp.broadcast_to(turned[:, c : c + 1], (width, LANES))
    pos, vel = centred(own_ref[0:6, :], mid_ref)
    rows_ref[...] = jnp.zeros(rows_ref.shape, f32)
    row = 0
    for high, mid, low in (three_parts(-vel), three_parts(-pos)):
        for x in (high, high, mid, high, mid, low):
            rows_ref[row : row + 3, :] = x
            row += 3
    rows_ref[row : row + 3, :] = jnp.ones((3, width), f32)
    for i, x in enumerate(dot_parts(pos, vel)):
        rows_ref[row + 3 + i : row + 4 + i, :] = x
    near_feat[...] = jnp.transpose(rows_ref[...])


def set_sources(src_ref, mid_ref, feat, right, far_feat, width):
    count = feat.shape[2]
    pos, vel = centred(src_ref[0:6, 0:count], mid_ref)
    pos_parts = three_parts(pos)
    vel_parts = three_parts(vel)
    one = jnp.ones((3, count), f32)
    feat[...] = jnp.zeros(feat.shape, f32)
    for i, x in enumerate((*pos_parts, *vel_parts)):
        feat[0, 3 * i : 3 * i + 3, :] = x
    feat[0, 18:19, :] = one[0:1, :]
    for i, x in enumerate(pos_parts):
        feat[1, 32 + 3 * i : 35 + 3 * i, :] = x
    feat[1, 41:42, :] = one[0:1, :]
    row = 0
    for high, mid, low in (pos_parts, vel_parts):
        for x in (high, mid, high, low, mid, high):
            feat[2, row : row + 3, :] = x
            row += 3
    for i, x in enumerate(dot_parts(pos, vel)):
        feat[2, row + i : row + i + 1, :] = x
    feat[2, row + 3 : row + 6, :] = one
    for k in range(right.shape[0]):
        cs = slice(k * width, k * width + width)
        for i in range(4):
            right[k, :, i * width : i * width + width] = feat[i // 2, :, cs].astype(bf16)
        far_feat[k] = feat[2, :, cs].astype(bf16)


def pair_chunk(source, offset, flow, wide, left, pot_ref, shift):
    width = wide.shape[1]
    for rb in range(width // ROWS):
        rs = slice(rb * ROWS, rb * ROWS + ROWS)
        target = [wide[c, rs, :] for c in range(3)]
        pot = pot_ref[rs, :]
        for j in range(width // LANES):
            cs = slice(offset + LANES * j, offset + LANES * j + LANES)
            dx, dy, dz = (
                jnp.broadcast_to(source[c : c + 1, cs], (ROWS, LANES)) - target[c] for c in range(3)
            )
            inverse = lax.rsqrt(((dx * dx + soften) + dy * dy) + dz * dz)
            inv_sq = inverse * inverse
            weighted = jnp.broadcast_to(source[6:7, cs], (ROWS, LANES)) * inverse
            pot = pot + weighted
            cube = weighted * inv_sq
            if shift is not None and rb * ROWS // LANES == j:
                here = lax.broadcasted_iota(jnp.int32, (ROWS, LANES), 0) + (rb * ROWS - j * LANES + shift)
                there = lax.broadcasted_iota(jnp.int32, (ROWS, LANES), 1)
                cube = jnp.where(here == there, 0.0, cube)
            radial = cube * (flow[rs, LANES * j : LANES * j + LANES] * inv_sq)
            parts = (
                cube,
                cube - cube.astype(bf16).astype(f32),
                radial,
                radial - radial.astype(bf16).astype(f32),
            )
            for i, x in enumerate(parts):
                left[rs, i * width + LANES * j : i * width + LANES * j + LANES] = x
        pot_ref[rs, :] = pot


def add_chunk(left, right, sum_ref):
    sum_ref[...] += lax.dot_general(left[...].astype(bf16), right, BOTH_MINOR, preferred_element_type=f32)


def pair_block(source, wide, near_feat, sum_ref, pot_ref, right, far_feat, left, flow, own_block):
    width = wide.shape[1]
    chunks = right.shape[0]
    rank = lax.axis_index("ia")
    mine = near_feat[...].astype(bf16)

    def set_flow(k):
        flow[k % 2] = jnp.dot(mine, far_feat[k], preferred_element_type=f32)

    set_flow(0)
    for k in range(chunks):
        if k + 1 < chunks:
            set_flow(k + 1)
        if k:
            add_chunk(left.at[(k - 1) % 2], right[k - 1], sum_ref)
        shift = jnp.where(rank == k, 0, width) if own_block else None
        pair_chunk(source, k * width, flow.at[k % 2], wide, left.at[k % 2], pot_ref, shift)
    add_chunk(left.at[(chunks - 1) % 2], right[chunks - 1], sum_ref)


def near_kernel(src_ref, own_ref, mid_ref, sum_ref, pot_ref, wide, near_feat, *work):
    feat, right, far_feat, left, flow, rows_ref = work
    set_targets(own_ref, mid_ref, wide, near_feat, rows_ref)
    set_sources(src_ref, mid_ref, feat, right, far_feat, own_ref.shape[1])
    sum_ref[...] = jnp.zeros(sum_ref.shape, f32)
    pot_ref[...] = jnp.zeros(pot_ref.shape, f32)
    pair_block(src_ref, wide, near_feat, sum_ref, pot_ref, right, far_feat, left, flow, True)


def twin_kernel(count, *refs):
    blocks = refs[:count]
    src_ref, mid_ref, wide, near_feat, sum_in, pot_in = refs[count : count + 6]
    sum_ref, pot_ref, other_sum, other_pot, other_own, other_wide, other_feat = refs[count + 6 : count + 13]
    feat, right, far_feat, left, flow, rows_ref = refs[count + 13 :]
    width = wide.shape[1]
    stars = src_ref.shape[1]
    mine = pl.ds(pl.multiple_of(lax.axis_index("ia") * width, LANES), width)
    other_own[0:8, :] = blocks[-1][:, mine]
    other_own[8:16, :] = blocks[-1][:, stars : stars + width]
    set_targets(other_own, mid_ref, other_wide, other_feat, rows_ref)
    sum_ref[...] = sum_in[...]
    pot_ref[...] = pot_in[...]
    other_sum[...] = jnp.zeros(other_sum.shape, f32)
    other_pot[...] = jnp.zeros(other_pot.shape, f32)
    for i, block in enumerate((*blocks, src_ref)):
        set_sources(block, mid_ref, feat, right, far_feat, width)
        if i < count:
            pair_block(block, wide, near_feat, sum_ref, pot_ref, right, far_feat, left, flow, False)
        pair_block(
            block, other_wide, other_feat, other_sum, other_pot, right, far_feat, left, flow, i == count - 1
        )


def finish(own_ref, mid_ref, sum_ref, pot_ref, out_ref, cs):
    width = own_ref.shape[1]
    sums = jnp.transpose(sum_ref[...])
    pot = jnp.sum(jnp.transpose(pot_ref[...]), axis=0, keepdims=True)
    near_pos, near_vel = centred(own_ref[0:6, :], mid_ref)
    total = sums[18:19, :]
    new_acc = (sums[0:3, :] - near_pos * total) + sums[3:6, :] + sums[6:9, :]
    drift = (sums[9:12, :] - near_vel * total) + sums[12:15, :] + sums[15:18, :]
    pull = (sums[32:35, :] - near_pos * sums[41:42, :]) + sums[35:38, :] + sums[38:41, :]
    new_jolt = drift - 3.0 * pull
    position, velocity = correct(
        own_ref[0:3, :], own_ref[3:6, :], own_ref[8:11, :], own_ref[11:14, :], own_ref[7:8, :], new_acc, new_jolt
    )
    out_ref[0:3, cs] = position
    out_ref[3:6, cs] = velocity
    out_ref[6:8, cs] = jnp.zeros((2, width), f32)
    out_ref[8:11, cs] = new_acc
    out_ref[11:14, cs] = new_jolt
    out_ref[14:15, cs] = -pot
    out_ref[15:16, cs] = jnp.zeros((1, width), f32)


def last_kernel(count, *refs):
    blocks = refs[:count]
    mid_ref = refs[count]
    sets = (refs[count + 1 : count + 6], refs[count + 6 : count + 11])
    out_ref = refs[count + 11]
    totals = (refs[count + 12 : count + 14], refs[count + 14 : count + 16])
    feat, right, far_feat, left, flow, rows_ref = refs[count + 16 :]
    for (own_ref, wide, near_feat, sum_in, pot_in), (sum_ref, pot_ref) in zip(sets, totals):
        sum_ref[...] = sum_in[...]
        pot_ref[...] = pot_in[...]
    width = sets[0][0].shape[1]
    for block in blocks:
        set_sources(block, mid_ref, feat, right, far_feat, width)
        for (own_ref, wide, near_feat, sum_in, pot_in), (sum_ref, pot_ref) in zip(sets, totals):
            pair_block(block, wide, near_feat, sum_ref, pot_ref, right, far_feat, left, flow, False)
    for i, ((own_ref, wide, near_feat, sum_in, pot_in), (sum_ref, pot_ref)) in enumerate(zip(sets, totals)):
        finish(own_ref, mid_ref, sum_ref, pot_ref, out_ref, slice(i * width, i * width + width))


def pick_kernel(ia_bits, ja_bits, width, first_slot, last, refs):
    table_ref, local_ref, owner_ref = refs[:3]
    before = refs[3:-2]
    state_ref, forces_ref = refs[-2:]
    count = local_ref.shape[0]
    per = width // LANES
    my_ja = lax.axis_index("ja")
    my_ia = lax.axis_index("ia")
    for b in range(count // LANES):
        cs = slice(b * LANES, b * LANES + LANES)
        local = local_ref[cs].reshape(1, LANES)
        apart_ja = lax.bitwise_xor(owner_ref[cs].reshape(1, LANES), my_ja)
        apart_ia = lax.bitwise_xor(local // width, my_ia)
        step = lax.bitwise_and(apart_ja, (1 << (ja_bits - 1)) - 1)
        flips = apart_ia + (step != 0).astype(jnp.int32)
        for i in range(1, ia_bits):
            flips = flips + lax.shift_right_logical(apart_ia, i)
        slot = step + step + lax.shift_right_logical(apart_ja, ja_bits - 1)
        slot = slot + lax.shift_left(lax.shift_right_logical(apart_ia, 1), ja_bits)
        slot = slot + lax.shift_left(lax.bitwise_and(flips, 1), ja_bits + ia_bits - 1)
        within = lax.rem(local, width)
        piece = jnp.broadcast_to((slot - first_slot) * per + within // LANES, (8, LANES))
        lane = jnp.broadcast_to(lax.rem(within, LANES), (8, LANES))
        state = before[0][:, cs] if before else jnp.zeros((8, LANES), f32)
        forces = before[1][:, cs] if before else jnp.zeros((8, LANES), f32)
        for t in range(table_ref.shape[1] // LANES):
            hit = piece == t
            ts = slice(t * LANES, t * LANES + LANES)
            state = jnp.where(hit, jnp.take_along_axis(table_ref[0:8, ts], lane, axis=1), state)
            forces = jnp.where(hit, jnp.take_along_axis(table_ref[8:16, ts], lane, axis=1), forces)
        state_ref[:, cs] = state[0 : state_ref.shape[0], :]
        forces_ref[:, cs] = forces[0 : forces_ref.shape[0], :]


def shape_of(*dims):
    return jax.ShapeDtypeStruct(dims, f32)


def all_stars(nj, ni, pos_vel, acc_jerk, mass, age, active_local, active_owner):
    stars = mass.shape[0]
    width = stars // ni
    chunks = stars // width
    ja_bits = nj.bit_length() - 1
    ia_bits = ni.bit_length() - 1

    def exchange(x, dj, di):
        pairs = [(j * ni + i, (j ^ dj) * ni + (i ^ di)) for j in range(nj) for i in range(ni)]
        return lax.ppermute(x, ("ja", "ia"), pairs)

    twin = nj // 2
    src, long, own, mid = pl.pallas_call(
        predict_kernel,
        out_shape=(shape_of(8, stars), shape_of(8, stars + width), shape_of(16, width), shape_of(8, LANES)),
        in_specs=[pl.BlockSpec(memory_space=pltpu.HBM)] * 4,
        out_specs=(VMEM,) * 4,
        scratch_shapes=[
            pltpu.VMEM((6, stars), f32),
            pltpu.VMEM((6, stars), f32),
            pltpu.VMEM((1, stars), f32),
            pltpu.VMEM((1, stars), f32),
            pltpu.SemaphoreType.DMA((4,)),
        ],
        compiler_params=PARAMS,
        name="predict",
    )(*(pltpu.with_memory_space_constraint(x, pltpu.HBM) for x in (pos_vel, acc_jerk, mass[None, :], age[None, :])))
    others = [exchange(long if d == twin else src, d, 1) for d in range(1, nj)]
    scratch = [
        pltpu.VMEM((3, COLS, stars), f32),
        pltpu.VMEM((chunks, COLS, 4 * width), bf16),
        pltpu.VMEM((chunks, COLS, width), bf16),
        pltpu.VMEM((2, width, 4 * width), f32),
        pltpu.VMEM((2, width, width), f32),
        pltpu.VMEM((COLS, width), f32),
    ]
    held = (shape_of(width, COLS), shape_of(width, LANES))
    aims = (shape_of(3, width, LANES), shape_of(width, COLS))

    def call(kernel, name, blocks, out_shape, more, args):
        single = not isinstance(out_shape, tuple)
        return pl.pallas_call(
            kernel,
            out_shape=out_shape,
            in_specs=[VMEM] * len(args),
            out_specs=VMEM if single else (VMEM,) * len(out_shape),
            scratch_shapes=more + scratch,
            compiler_params=PARAMS,
            cost_estimate=pl.CostEstimate(
                flops=blocks * 40 * width * stars, transcendentals=blocks * width * stars, bytes_accessed=400000
            ),
            name=name,
        )(*args)

    sums, pot, wide, feat = call(near_kernel, "near", 1, held + aims, [], (src, own, mid))
    sums, pot, other_sums, other_pot, other_own, other_wide, other_feat = call(
        lambda *refs: twin_kernel(twin, *refs),
        "twin",
        2 * twin + 1,
        held + held + (shape_of(16, width),) + aims,
        [],
        (*others[:twin], src, mid, wide, feat, sums, pot),
    )
    block = call(
        lambda *refs: last_kernel(nj - 1 - twin, *refs),
        "last",
        2 * (nj - 1 - twin),
        shape_of(16, 2 * width),
        [pltpu.VMEM(x.shape, f32) for x in held + held],
        (*others[twin:], mid, own, wide, feat, sums, pot, other_own, other_wide, other_feat, other_sums, other_pot),
    )
    count = active_local.shape[0]

    def pick(table, first_slot, before, last=False):
        return pl.pallas_call(
            lambda *refs: pick_kernel(ia_bits, ja_bits, width, first_slot, last, refs),
            out_shape=(shape_of(6 if last else 8, count), shape_of(7 if last else 8, count)),
            in_specs=[VMEM] * (3 + len(before)),
            out_specs=(VMEM, VMEM),
            compiler_params=PARAMS,
            cost_estimate=pl.CostEstimate(flops=count * table.shape[1], transcendentals=0, bytes_accessed=400000),
            name="pick",
        )(table, active_local, active_owner, *before)

    table = jnp.concatenate([block, *(exchange(block, d, 1) for d in range(1, twin))], axis=1)
    half = 1 << (ja_bits + ia_bits - 1)
    tables = [(0, table)]
    came = [(half, exchange(table, 0, 1))]
    for bit in range(1, ia_bits):
        for slot, there in list(tables):
            fresh = exchange(there, 0, (1 << bit) + 1)
            new_slot = slot + (nj << (bit - 1))
            tables.append((new_slot, fresh))
            came.append((half + new_slot, exchange(fresh, 0, 1)))
    order = [tables[0], came[0]]
    for pair in zip(tables[1:], came[1:]):
        order.extend(pair)
    found = ()
    for i, (slot, there) in enumerate(order):
        found = pick(there, slot, found, i == len(order) - 1)
    return found


def solution(mesh):
    nj = mesh.shape["ja"]
    ni = mesh.shape["ia"]

    def local(pos_vel, acc_jerk, mass, age, active_local, active_owner):
        stars = mass.shape[0]
        width = stars // ni
        fits = (
            nj & (nj - 1) == 0
            and ni & (ni - 1) == 0
            and 1 < nj <= 8
            and ni > 1
            and stars % ni == 0
            and width % LANES == 0
            and width <= 256
            and active_local.shape[0] % LANES == 0
            and stars * nj <= active_local.shape[0] * ni
        )
        args = (pos_vel, acc_jerk, mass, age, active_local, active_owner)
        return all_stars(nj, ni, *args) if fits else general(*args)

    return jax.shard_map(
        local,
        mesh=mesh,
        in_specs=(
            P(None, ("grp", "ja")),
            P(None, ("grp", "ja")),
            P(("grp", "ja")),
            P(("grp", "ja")),
            P(("grp", "ia")),
            P(("grp", "ia")),
        ),
        out_specs=(P(None, ("grp", "ia")), P(None, ("grp", "ia"))),
        check_vma=False,
    )
```

```python
import jax
import jax.numpy as jnp
from jax import lax
from jax.experimental import pallas as pl
from jax.experimental.pallas import tpu as pltpu
from jax.sharding import PartitionSpec as P

soften = 0.0004
f32 = jnp.float32
bf16 = jnp.bfloat16
LANES = 128
ROWS = 16
COLS = 48
VMEM = pl.BlockSpec(memory_space=pltpu.VMEM)
PARAMS = pltpu.CompilerParams(vmem_limit_bytes=16 << 20)
BOTH_MINOR = (((1,), (1,)), ((), ()))


def predict(pos_vel, acc_jerk, age):
    position = pos_vel[0:3]
    velocity = pos_vel[3:6]
    accel = acc_jerk[0:3]
    jolt = acc_jerk[3:6]
    step_len = age[None, :]
    new_pos = position + step_len * (velocity + step_len * (accel * 0.5 + step_len * jolt / 6.0))
    new_vel = velocity + step_len * (accel + step_len * jolt * 0.5)
    return jnp.concatenate([new_pos, new_vel], axis=0)


def pair_terms(targets, sources, masses):
    delta_pos = sources[0:3, :, None] - targets[0:3, None, :]
    delta_vel = sources[3:6, :, None] - targets[3:6, None, :]
    dist_sq = jnp.sum(delta_pos * delta_pos, axis=0) + soften
    inverse = lax.rsqrt(dist_sq)
    inv_sq = inverse * inverse
    weighted = masses[:, None] * inverse
    weighted_cube = weighted * inv_sq
    radial = 3.0 * jnp.sum(delta_pos * delta_vel, axis=0) * inv_sq
    accel = jnp.sum(weighted_cube[None] * delta_pos, axis=1)
    jolt = jnp.sum(weighted_cube[None] * (delta_vel - radial[None] * delta_pos), axis=1)
    potential = -jnp.sum(weighted, axis=0)
    return jnp.concatenate([accel, jolt, potential[None]], axis=0)


def block_terms(targets, sources, masses):
    count = targets.shape[1]
    width = min(512, count)
    nblocks = count // width
    src_count = sources.shape[1]
    src_width = min(512, src_count)
    src_blocks = src_count // src_width
    source_pieces = sources.reshape(6, src_blocks, src_width).transpose(1, 0, 2)
    mass_pieces = masses.reshape(src_blocks, src_width)
    pieces = targets.reshape(6, nblocks, width).transpose(1, 0, 2)

    def one_block(piece):

        def accumulate(total, parts):
            return (total + pair_terms(piece, parts[0], parts[1]), None)

        total, unused = lax.scan(
            accumulate, jnp.zeros((7, width), jnp.float32), (source_pieces, mass_pieces)
        )
        return total

    results = lax.map(one_block, pieces)
    return results.transpose(1, 0, 2).reshape(7, count)


def correct(pred_pos, pred_vel, old_acc, old_jolt, step_len, new_acc, new_jolt):
    differ = old_acc - new_acc
    square = step_len * step_len
    cubed = square * step_len
    fourth = square * square
    fifth = fourth * step_len
    second = (-6.0 * differ - step_len * (4.0 * old_jolt + 2.0 * new_jolt)) / square
    third = (12.0 * differ + 6.0 * step_len * (old_jolt + new_jolt)) / cubed
    position = pred_pos + fourth / 24.0 * second + fifth / 120.0 * third
    velocity = pred_vel + cubed / 6.0 * second + fourth / 24.0 * third
    return position, velocity


def general(pos_vel, acc_jerk, mass, age, active_local, active_owner):
    shard_rank = lax.axis_index("ja")
    predicted = predict(pos_vel, acc_jerk, age)
    stacked = jnp.concatenate([predicted, acc_jerk, age[None, :]], axis=0)
    picked = jnp.take(stacked, active_local, axis=1)
    owned = active_owner == shard_rank
    contrib = jnp.where(owned[None, :], picked, 0.0)
    history = lax.psum(contrib, "ja")
    partial_value = block_terms(history[0:6], predicted, mass)
    forces = lax.psum(partial_value, "ja")
    position, velocity = correct(
        history[0:3], history[3:6], history[6:9], history[9:12], history[12:13], forces[0:3], forces[3:6]
    )
    return (jnp.concatenate([position, velocity], axis=0), forces)


def predict_kernel(pv_hbm, aj_hbm, mass_hbm, age_hbm, src_ref, long_ref, own_ref, mid_ref, pv_ref, aj_ref, mass_ref, age_ref, sems):
    copies = [
        pltpu.make_async_copy(hbm, ref, sems.at[i])
        for i, (hbm, ref) in enumerate(
            ((pv_hbm, pv_ref), (aj_hbm, aj_ref), (mass_hbm, mass_ref), (age_hbm, age_ref))
        )
    ]
    for copy in copies:
        copy.start()
    for copy in copies:
        copy.wait()
    width = own_ref.shape[1]
    stars = src_ref.shape[1]
    step_len = age_ref[...]
    accel = aj_ref[0:3, :]
    jolt = aj_ref[3:6, :]
    velocity = pv_ref[3:6, :]
    src_ref[0:3, :] = pv_ref[0:3, :] + step_len * (velocity + step_len * (accel * 0.5 + step_len * jolt / 6.0))
    src_ref[3:6, :] = velocity + step_len * (accel + step_len * jolt * 0.5)
    src_ref[6:7, :] = mass_ref[...]
    src_ref[7:8, :] = step_len
    long_ref[:, 0:stars] = src_ref[...]
    rank = lax.axis_index("ia")
    mine = pl.ds(pl.multiple_of(rank * width, LANES), width)
    partner = pl.ds(pl.multiple_of(lax.bitwise_xor(rank, 1) * width, LANES), width)
    long_ref[0:6, stars : stars + width] = aj_ref[:, partner]
    long_ref[6:8, stars : stars + width] = jnp.zeros((2, width), f32)
    own_ref[0:8, :] = src_ref[:, mine]
    own_ref[8:14, :] = aj_ref[:, mine]
    own_ref[14:16, :] = jnp.zeros((2, width), f32)
    mean = jnp.sum(src_ref[:, mine], axis=1, keepdims=True) * (1.0 / width)
    mid_ref[...] = jnp.broadcast_to(mean, (8, LANES))


def three_parts(x):
    high = x.astype(bf16).astype(f32)
    rest = x - high
    mid = rest.astype(bf16).astype(f32)
    return high, mid, rest - mid


def centred(rows, mid_ref):
    middle = jnp.concatenate([mid_ref[...]] * (rows.shape[1] // LANES), axis=1)
    return rows[0:3, :] - middle[0:3, :], rows[3:6, :] - middle[3:6, :]


def dot_parts(a, b):
    return three_parts(jnp.sum(a * b, axis=0, keepdims=True))


def set_constants(feat, rows_ref):
    feat[...] = jnp.zeros(feat.shape, f32)
    rows_ref[...] = jnp.zeros(rows_ref.shape, f32)
    one = jnp.ones((3, feat.shape[2]), f32)
    feat[0, 18:19, :] = one[0:1, :]
    feat[1, 33:34, :] = one[0:1, :]
    feat[2, 39:42, :] = one
    rows_ref[36:39, :] = one[:, 0 : rows_ref.shape[1]]


def set_targets(own_ref, mid_ref, wide, near_feat, rows_ref):
    width = own_ref.shape[1]
    turned = jnp.transpose(own_ref[0:8, :])
    for c in range(3):
        wide[c] = jnp.broadcast_to(turned[:, c : c + 1], (width, LANES))
    pos, vel = centred(own_ref[0:6, :], mid_ref)
    row = 0
    for high, mid, low in (three_parts(-vel), three_parts(-pos)):
        for x in (high, high, mid, high, mid, low):
            rows_ref[row : row + 3, :] = x
            row += 3
    for i, x in enumerate(dot_parts(pos, vel)):
        rows_ref[row + 3 + i : row + 4 + i, :] = x
    near_feat[...] = jnp.transpose(rows_ref[...])


def set_sources(src_ref, mid_ref, feat, right, far_feat, width):
    count = feat.shape[2]
    pos, vel = centred(src_ref[0:6, 0:count], mid_ref)
    pos_parts = three_parts(pos)
    vel_parts = three_parts(vel)
    for i, x in enumerate((*pos_parts, *vel_parts)):
        feat[0, 3 * i : 3 * i + 3, :] = x
    for i, x in enumerate(pos_parts):
        feat[1, 24 + 3 * i : 27 + 3 * i, :] = x
    row = 0
    for high, mid, low in (pos_parts, vel_parts):
        for x in (high, mid, high, low, mid, high):
            feat[2, row : row + 3, :] = x
            row += 3
    for i, x in enumerate(dot_parts(pos, vel)):
        feat[2, row + i : row + i + 1, :] = x
    for k in range(right.shape[0]):
        cs = slice(k * width, k * width + width)
        for i in range(4):
            right[k, :, i * width : i * width + width] = feat[i // 2, :, cs].astype(bf16)
        far_feat[k] = feat[2, :, cs].astype(bf16)


def pair_chunk(source, offset, flow, wide, left, pot_ref, shift):
    width = wide.shape[1]
    for j in range(width // LANES):
        cs = slice(offset + LANES * j, offset + LANES * j + LANES)
        source_rows = [jnp.broadcast_to(source[c : c + 1, cs], (ROWS, LANES)) for c in (0, 1, 2, 6)]
        for rb in range(width // ROWS):
            rs = slice(rb * ROWS, rb * ROWS + ROWS)
            dx, dy, dz = (source_rows[c] - wide[c, rs, :] for c in range(3))
            inverse = lax.rsqrt(((dx * dx + soften) + dy * dy) + dz * dz)
            inv_sq = inverse * inverse
            weighted = source_rows[3] * inverse
            pot_ref[rs, :] += weighted
            cube = weighted * inv_sq
            if shift is not None and rb * ROWS // LANES == j:
                here = lax.broadcasted_iota(jnp.int32, (ROWS, LANES), 0) + (rb * ROWS - j * LANES + shift)
                there = lax.broadcasted_iota(jnp.int32, (ROWS, LANES), 1)
                cube = jnp.where(here == there, 0.0, cube)
            radial = cube * (flow[rs, LANES * j : LANES * j + LANES] * inv_sq)
            parts = (
                cube,
                cube - cube.astype(bf16).astype(f32),
                radial,
                radial - radial.astype(bf16).astype(f32),
            )
            for i, x in enumerate(parts):
                left[rs, i * width + LANES * j : i * width + LANES * j + LANES] = x


def add_chunk(left, right, sum_ref):
    sum_ref[...] += lax.dot_general(left[...].astype(bf16), right, BOTH_MINOR, preferred_element_type=f32)


def pair_block(source, wide, near_feat, sum_ref, pot_ref, right, far_feat, left, flow, own_block):
    width = wide.shape[1]
    chunks = right.shape[0]
    rank = lax.axis_index("ia")
    mine = near_feat[...].astype(bf16)

    def set_flow(k):
        flow[k % 2] = jnp.dot(mine, far_feat[k], preferred_element_type=f32)

    set_flow(0)
    for k in range(chunks):
        if k + 1 < chunks:
            set_flow(k + 1)
        if k:
            add_chunk(left.at[(k - 1) % 2], right[k - 1], sum_ref)
        shift = jnp.where(rank == k, 0, width) if own_block else None
        pair_chunk(source, k * width, flow.at[k % 2], wide, left.at[k % 2], pot_ref, shift)
    add_chunk(left.at[(chunks - 1) % 2], right[chunks - 1], sum_ref)


def near_kernel(src_ref, own_ref, mid_ref, sum_ref, pot_ref, wide, near_feat, *work):
    feat, right, far_feat, left, flow, rows_ref = work
    set_constants(feat, rows_ref)
    set_targets(own_ref, mid_ref, wide, near_feat, rows_ref)
    set_sources(src_ref, mid_ref, feat, right, far_feat, own_ref.shape[1])
    sum_ref[...] = jnp.zeros(sum_ref.shape, f32)
    pot_ref[...] = jnp.zeros(pot_ref.shape, f32)
    pair_block(src_ref, wide, near_feat, sum_ref, pot_ref, right, far_feat, left, flow, True)


def twin_kernel(count, *refs):
    blocks = refs[:count]
    src_ref, mid_ref, wide, near_feat, sum_in, pot_in = refs[count : count + 6]
    sum_ref, pot_ref, other_sum, other_pot, other_own, other_wide, other_feat = refs[count + 6 : count + 13]
    feat, right, far_feat, left, flow, rows_ref = refs[count + 13 :]
    width = wide.shape[1]
    stars = src_ref.shape[1]
    mine = pl.ds(pl.multiple_of(lax.axis_index("ia") * width, LANES), width)
    other_own[0:8, :] = blocks[-1][:, mine]
    other_own[8:16, :] = blocks[-1][:, stars : stars + width]
    set_constants(feat, rows_ref)
    set_targets(other_own, mid_ref, other_wide, other_feat, rows_ref)
    sum_ref[...] = sum_in[...]
    pot_ref[...] = pot_in[...]
    other_sum[...] = jnp.zeros(other_sum.shape, f32)
    other_pot[...] = jnp.zeros(other_pot.shape, f32)
    for i, block in enumerate((*blocks, src_ref)):
        set_sources(block, mid_ref, feat, right, far_feat, width)
        if i < count:
            pair_block(block, wide, near_feat, sum_ref, pot_ref, right, far_feat, left, flow, False)
        pair_block(
            block, other_wide, other_feat, other_sum, other_pot, right, far_feat, left, flow, i == count - 1
        )


def finish(own_ref, mid_ref, sum_ref, pot_ref, out_ref, cs):
    width = own_ref.shape[1]
    sums = jnp.transpose(sum_ref[...])
    pot = jnp.sum(jnp.transpose(pot_ref[...]), axis=0, keepdims=True)
    near_pos, near_vel = centred(own_ref[0:6, :], mid_ref)
    total = sums[18:19, :]
    new_acc = (sums[0:3, :] - near_pos * total) + sums[3:6, :] + sums[6:9, :]
    drift = (sums[9:12, :] - near_vel * total) + sums[12:15, :] + sums[15:18, :]
    pull = (sums[24:27, :] - near_pos * sums[33:34, :]) + sums[27:30, :] + sums[30:33, :]
    new_jolt = drift - 3.0 * pull
    position, velocity = correct(
        own_ref[0:3, :], own_ref[3:6, :], own_ref[8:11, :], own_ref[11:14, :], own_ref[7:8, :], new_acc, new_jolt
    )
    out_ref[0:3, cs] = position
    out_ref[3:6, cs] = velocity
    out_ref[6:8, cs] = jnp.zeros((2, width), f32)
    out_ref[8:11, cs] = new_acc
    out_ref[11:14, cs] = new_jolt
    out_ref[14:15, cs] = -pot
    out_ref[15:16, cs] = jnp.zeros((1, width), f32)


def last_kernel(count, *refs):
    blocks = refs[:count]
    mid_ref = refs[count]
    sets = (refs[count + 1 : count + 6], refs[count + 6 : count + 11])
    out_ref = refs[count + 11]
    totals = (refs[count + 12 : count + 14], refs[count + 14 : count + 16])
    feat, right, far_feat, left, flow, rows_ref = refs[count + 16 :]
    set_constants(feat, rows_ref)
    for (own_ref, wide, near_feat, sum_in, pot_in), (sum_ref, pot_ref) in zip(sets, totals):
        sum_ref[...] = sum_in[...]
        pot_ref[...] = pot_in[...]
    width = sets[0][0].shape[1]
    for block in blocks:
        set_sources(block, mid_ref, feat, right, far_feat, width)
        for (own_ref, wide, near_feat, sum_in, pot_in), (sum_ref, pot_ref) in zip(sets, totals):
            pair_block(block, wide, near_feat, sum_ref, pot_ref, right, far_feat, left, flow, False)
    for i, ((own_ref, wide, near_feat, sum_in, pot_in), (sum_ref, pot_ref)) in enumerate(zip(sets, totals)):
        finish(own_ref, mid_ref, sum_ref, pot_ref, out_ref, slice(i * width, i * width + width))


def pick_kernel(ia_bits, ja_bits, width, first_slot, last, refs):
    table_ref, local_ref, owner_ref = refs[:3]
    before = refs[3:-2]
    state_ref, forces_ref = refs[-2:]
    count = local_ref.shape[0]
    per = width // LANES
    my_ja = lax.axis_index("ja")
    my_ia = lax.axis_index("ia")
    for b in range(count // LANES):
        cs = slice(b * LANES, b * LANES + LANES)
        local = local_ref[cs].reshape(1, LANES)
        apart_ja = lax.bitwise_xor(owner_ref[cs].reshape(1, LANES), my_ja)
        apart_ia = lax.bitwise_xor(local // width, my_ia)
        step = lax.bitwise_and(apart_ja, (1 << (ja_bits - 1)) - 1)
        flips = apart_ia + (step != 0).astype(jnp.int32)
        for i in range(1, ia_bits):
            flips = flips + lax.shift_right_logical(apart_ia, i)
        slot = step + step + lax.shift_right_logical(apart_ja, ja_bits - 1)
        slot = slot + lax.shift_left(lax.shift_right_logical(apart_ia, 1), ja_bits)
        slot = slot + lax.shift_left(lax.bitwise_and(flips, 1), ja_bits + ia_bits - 1)
        within = lax.rem(local, width)
        piece = jnp.broadcast_to((slot - first_slot) * per + within // LANES, (8, LANES))
        lane = jnp.broadcast_to(lax.rem(within, LANES), (8, LANES))
        state = before[0][:, cs] if before else jnp.zeros((8, LANES), f32)
        forces = before[1][:, cs] if before else jnp.zeros((8, LANES), f32)
        for t in range(table_ref.shape[1] // LANES):
            hit = piece == t
            ts = slice(t * LANES, t * LANES + LANES)
            state = jnp.where(hit, jnp.take_along_axis(table_ref[0:8, ts], lane, axis=1), state)
            forces = jnp.where(hit, jnp.take_along_axis(table_ref[8:16, ts], lane, axis=1), forces)
        state_ref[:, cs] = state[0 : state_ref.shape[0], :]
        forces_ref[:, cs] = forces[0 : forces_ref.shape[0], :]


def shape_of(*dims):
    return jax.ShapeDtypeStruct(dims, f32)


def all_stars(nj, ni, pos_vel, acc_jerk, mass, age, active_local, active_owner):
    stars = mass.shape[0]
    width = stars // ni
    chunks = stars // width
    ja_bits = nj.bit_length() - 1
    ia_bits = ni.bit_length() - 1

    def exchange(x, dj, di):
        pairs = [(j * ni + i, (j ^ dj) * ni + (i ^ di)) for j in range(nj) for i in range(ni)]
        return lax.ppermute(x, ("ja", "ia"), pairs)

    twin = nj // 2
    src, long, own, mid = pl.pallas_call(
        predict_kernel,
        out_shape=(shape_of(8, stars), shape_of(8, stars + width), shape_of(16, width), shape_of(8, LANES)),
        in_specs=[pl.BlockSpec(memory_space=pltpu.HBM)] * 4,
        out_specs=(VMEM,) * 4,
        scratch_shapes=[
            pltpu.VMEM((6, stars), f32),
            pltpu.VMEM((6, stars), f32),
            pltpu.VMEM((1, stars), f32),
            pltpu.VMEM((1, stars), f32),
            pltpu.SemaphoreType.DMA((4,)),
        ],
        compiler_params=PARAMS,
        name="predict",
    )(*(pltpu.with_memory_space_constraint(x, pltpu.HBM) for x in (pos_vel, acc_jerk, mass[None, :], age[None, :])))
    others = [exchange(long if d == twin else src, d, 1) for d in range(1, nj)]
    scratch = [
        pltpu.VMEM((3, COLS, stars), f32),
        pltpu.VMEM((chunks, COLS, 4 * width), bf16),
        pltpu.VMEM((chunks, COLS, width), bf16),
        pltpu.VMEM((2, width, 4 * width), f32),
        pltpu.VMEM((2, width, width), f32),
        pltpu.VMEM((COLS, width), f32),
    ]
    held = (shape_of(width, COLS), shape_of(width, LANES))
    aims = (shape_of(3, width, LANES), shape_of(width, COLS))

    def call(kernel, name, blocks, out_shape, more, args):
        single = not isinstance(out_shape, tuple)
        return pl.pallas_call(
            kernel,
            out_shape=out_shape,
            in_specs=[VMEM] * len(args),
            out_specs=VMEM if single else (VMEM,) * len(out_shape),
            scratch_shapes=more + scratch,
            compiler_params=PARAMS,
            cost_estimate=pl.CostEstimate(
                flops=blocks * 40 * width * stars, transcendentals=blocks * width * stars, bytes_accessed=400000
            ),
            name=name,
        )(*args)

    sums, pot, wide, feat = call(near_kernel, "near", 1, held + aims, [], (src, own, mid))
    sums, pot, other_sums, other_pot, other_own, other_wide, other_feat = call(
        lambda *refs: twin_kernel(twin, *refs),
        "twin",
        2 * twin + 1,
        held + held + (shape_of(16, width),) + aims,
        [],
        (*others[:twin], src, mid, wide, feat, sums, pot),
    )
    block = call(
        lambda *refs: last_kernel(nj - 1 - twin, *refs),
        "last",
        2 * (nj - 1 - twin),
        shape_of(16, 2 * width),
        [pltpu.VMEM(x.shape, f32) for x in held + held],
        (*others[twin:], mid, own, wide, feat, sums, pot, other_own, other_wide, other_feat, other_sums, other_pot),
    )
    count = active_local.shape[0]

    def pick(table, first_slot, before, last=False):
        return pl.pallas_call(
            lambda *refs: pick_kernel(ia_bits, ja_bits, width, first_slot, last, refs),
            out_shape=(shape_of(6 if last else 8, count), shape_of(7 if last else 8, count)),
            in_specs=[VMEM] * (3 + len(before)),
            out_specs=(VMEM, VMEM),
            compiler_params=PARAMS,
            cost_estimate=pl.CostEstimate(flops=count * table.shape[1], transcendentals=0, bytes_accessed=400000),
            name="pick",
        )(table, active_local, active_owner, *before)

    table = jnp.concatenate([block, *(exchange(block, d, 1) for d in range(1, twin))], axis=1)
    half = 1 << (ja_bits + ia_bits - 1)
    tables = [(0, table)]
    came = [(half, exchange(table, 0, 1))]
    for bit in range(1, ia_bits):
        for slot, there in list(tables):
            fresh = exchange(there, 0, (1 << bit) + 1)
            new_slot = slot + (nj << (bit - 1))
            tables.append((new_slot, fresh))
            came.append((half + new_slot, exchange(fresh, 0, 1)))
    order = [tables[0], came[0]]
    for pair in zip(tables[1:], came[1:]):
        order.extend(pair)
    found = ()
    for i, (slot, there) in enumerate(order):
        found = pick(there, slot, found, i == len(order) - 1)
    return found


def solution(mesh):
    nj = mesh.shape["ja"]
    ni = mesh.shape["ia"]

    def local(pos_vel, acc_jerk, mass, age, active_local, active_owner):
        stars = mass.shape[0]
        width = stars // ni
        fits = (
            nj & (nj - 1) == 0
            and ni & (ni - 1) == 0
            and 1 < nj <= 8
            and ni > 1
            and stars % ni == 0
            and width % LANES == 0
            and width <= 256
            and active_local.shape[0] % LANES == 0
            and stars * nj <= active_local.shape[0] * ni
        )
        args = (pos_vel, acc_jerk, mass, age, active_local, active_owner)
        return all_stars(nj, ni, *args) if fits else general(*args)

    return jax.shard_map(
        local,
        mesh=mesh,
        in_specs=(
            P(None, ("grp", "ja")),
            P(None, ("grp", "ja")),
            P(("grp", "ja")),
            P(("grp", "ja")),
            P(("grp", "ia")),
            P(("grp", "ia")),
        ),
        out_specs=(P(None, ("grp", "ia")), P(None, ("grp", "ia"))),
        check_vma=False,
    )
```

```python
import jax
import jax.numpy as jnp
from jax import lax
from jax.experimental import pallas as pl
from jax.experimental.pallas import tpu as pltpu
from jax.sharding import PartitionSpec as P

soften = 0.0004
f32 = jnp.float32
bf16 = jnp.bfloat16
LANES = 128
ROWS = 64
COLS = 48
VMEM = pl.BlockSpec(memory_space=pltpu.VMEM)
PARAMS = pltpu.CompilerParams(vmem_limit_bytes=16 << 20)
BOTH_MINOR = (((1,), (1,)), ((), ()))


def predict(pos_vel, acc_jerk, age):
    position = pos_vel[0:3]
    velocity = pos_vel[3:6]
    accel = acc_jerk[0:3]
    jolt = acc_jerk[3:6]
    step_len = age[None, :]
    new_pos = position + step_len * (velocity + step_len * (accel * 0.5 + step_len * jolt / 6.0))
    new_vel = velocity + step_len * (accel + step_len * jolt * 0.5)
    return jnp.concatenate([new_pos, new_vel], axis=0)


def pair_terms(targets, sources, masses):
    delta_pos = sources[0:3, :, None] - targets[0:3, None, :]
    delta_vel = sources[3:6, :, None] - targets[3:6, None, :]
    dist_sq = jnp.sum(delta_pos * delta_pos, axis=0) + soften
    inverse = lax.rsqrt(dist_sq)
    inv_sq = inverse * inverse
    weighted = masses[:, None] * inverse
    weighted_cube = weighted * inv_sq
    radial = 3.0 * jnp.sum(delta_pos * delta_vel, axis=0) * inv_sq
    accel = jnp.sum(weighted_cube[None] * delta_pos, axis=1)
    jolt = jnp.sum(weighted_cube[None] * (delta_vel - radial[None] * delta_pos), axis=1)
    potential = -jnp.sum(weighted, axis=0)
    return jnp.concatenate([accel, jolt, potential[None]], axis=0)


def block_terms(targets, sources, masses):
    count = targets.shape[1]
    width = min(512, count)
    nblocks = count // width
    src_count = sources.shape[1]
    src_width = min(512, src_count)
    src_blocks = src_count // src_width
    source_pieces = sources.reshape(6, src_blocks, src_width).transpose(1, 0, 2)
    mass_pieces = masses.reshape(src_blocks, src_width)
    pieces = targets.reshape(6, nblocks, width).transpose(1, 0, 2)

    def one_block(piece):

        def accumulate(total, parts):
            return (total + pair_terms(piece, parts[0], parts[1]), None)

        total, unused = lax.scan(
            accumulate, jnp.zeros((7, width), jnp.float32), (source_pieces, mass_pieces)
        )
        return total

    results = lax.map(one_block, pieces)
    return results.transpose(1, 0, 2).reshape(7, count)


def correct(pred_pos, pred_vel, old_acc, old_jolt, step_len, new_acc, new_jolt):
    differ = old_acc - new_acc
    square = step_len * step_len
    cubed = square * step_len
    fourth = square * square
    fifth = fourth * step_len
    second = (-6.0 * differ - step_len * (4.0 * old_jolt + 2.0 * new_jolt)) / square
    third = (12.0 * differ + 6.0 * step_len * (old_jolt + new_jolt)) / cubed
    position = pred_pos + fourth / 24.0 * second + fifth / 120.0 * third
    velocity = pred_vel + cubed / 6.0 * second + fourth / 24.0 * third
    return position, velocity


def general(pos_vel, acc_jerk, mass, age, active_local, active_owner):
    shard_rank = lax.axis_index("ja")
    predicted = predict(pos_vel, acc_jerk, age)
    stacked = jnp.concatenate([predicted, acc_jerk, age[None, :]], axis=0)
    picked = jnp.take(stacked, active_local, axis=1)
    owned = active_owner == shard_rank
    contrib = jnp.where(owned[None, :], picked, 0.0)
    history = lax.psum(contrib, "ja")
    partial_value = block_terms(history[0:6], predicted, mass)
    forces = lax.psum(partial_value, "ja")
    position, velocity = correct(
        history[0:3], history[3:6], history[6:9], history[9:12], history[12:13], forces[0:3], forces[3:6]
    )
    return (jnp.concatenate([position, velocity], axis=0), forces)


def predict_kernel(pv_hbm, aj_hbm, mass_hbm, age_hbm, src_ref, long_ref, own_ref, mid_ref, pv_ref, aj_ref, mass_ref, age_ref, sems):
    copies = [
        pltpu.make_async_copy(hbm, ref, sems.at[i])
        for i, (hbm, ref) in enumerate(
            ((pv_hbm, pv_ref), (aj_hbm, aj_ref), (mass_hbm, mass_ref), (age_hbm, age_ref))
        )
    ]
    for copy in copies:
        copy.start()
    for copy in copies:
        copy.wait()
    width = own_ref.shape[1]
    stars = src_ref.shape[1]
    step_len = age_ref[...]
    accel = aj_ref[0:3, :]
    jolt = aj_ref[3:6, :]
    velocity = pv_ref[3:6, :]
    src_ref[0:3, :] = pv_ref[0:3, :] + step_len * (velocity + step_len * (accel * 0.5 + step_len * jolt / 6.0))
    src_ref[3:6, :] = velocity + step_len * (accel + step_len * jolt * 0.5)
    src_ref[6:7, :] = mass_ref[...]
    src_ref[7:8, :] = step_len
    long_ref[:, 0:stars] = src_ref[...]
    rank = lax.axis_index("ia")
    mine = pl.ds(pl.multiple_of(rank * width, LANES), width)
    partner = pl.ds(pl.multiple_of(lax.bitwise_xor(rank, 1) * width, LANES), width)
    long_ref[0:6, stars : stars + width] = aj_ref[:, partner]
    long_ref[6:8, stars : stars + width] = jnp.zeros((2, width), f32)
    own_ref[0:8, :] = src_ref[:, mine]
    own_ref[8:14, :] = aj_ref[:, mine]
    own_ref[14:16, :] = jnp.zeros((2, width), f32)
    mean = jnp.sum(src_ref[:, mine], axis=1, keepdims=True) * (1.0 / width)
    mid_ref[...] = jnp.broadcast_to(mean, (8, LANES))


def three_parts(x):
    high = x.astype(bf16).astype(f32)
    rest = x - high
    mid = rest.astype(bf16).astype(f32)
    return high, mid, rest - mid


def centred(rows, mid_ref):
    middle = jnp.concatenate([mid_ref[...]] * (rows.shape[1] // LANES), axis=1)
    return rows[0:3, :] - middle[0:3, :], rows[3:6, :] - middle[3:6, :]


def dot_parts(a, b):
    return three_parts(jnp.sum(a * b, axis=0, keepdims=True))


def set_constants(feat, rows_ref):
    feat[...] = jnp.zeros(feat.shape, f32)
    rows_ref[...] = jnp.zeros(rows_ref.shape, f32)
    one = jnp.ones((3, feat.shape[2]), f32)
    feat[0, 18:19, :] = one[0:1, :]
    feat[1, 33:34, :] = one[0:1, :]
    feat[2, 39:42, :] = one
    rows_ref[36:39, :] = one[:, 0 : rows_ref.shape[1]]


def set_targets(own_ref, mid_ref, wide, near_feat, rows_ref):
    width = own_ref.shape[1]
    turned = jnp.transpose(own_ref[0:8, :])
    for c in range(3):
        wide[c] = jnp.broadcast_to(turned[:, c : c + 1], (width, LANES))
    pos, vel = centred(own_ref[0:6, :], mid_ref)
    row = 0
    for high, mid, low in (three_parts(-vel), three_parts(-pos)):
        for x in (high, high, mid, high, mid, low):
            rows_ref[row : row + 3, :] = x
            row += 3
    for i, x in enumerate(dot_parts(pos, vel)):
        rows_ref[row + 3 + i : row + 4 + i, :] = x
    near_feat[...] = jnp.transpose(rows_ref[...])


def set_sources(src_ref, mid_ref, feat, right, far_feat, width):
    count = feat.shape[2]
    pos, vel = centred(src_ref[0:6, 0:count], mid_ref)
    pos_parts = three_parts(pos)
    vel_parts = three_parts(vel)
    for i, x in enumerate((*pos_parts, *vel_parts)):
        feat[0, 3 * i : 3 * i + 3, :] = x
    for i, x in enumerate(pos_parts):
        feat[1, 24 + 3 * i : 27 + 3 * i, :] = x
    row = 0
    for high, mid, low in (pos_parts, vel_parts):
        for x in (high, mid, high, low, mid, high):
            feat[2, row : row + 3, :] = x
            row += 3
    for i, x in enumerate(dot_parts(pos, vel)):
        feat[2, row + i : row + i + 1, :] = x
    for k in range(right.shape[0]):
        cs = slice(k * width, k * width + width)
        for i in range(4):
            right[k, :, i * width : i * width + width] = feat[i // 2, :, cs].astype(bf16)
        far_feat[k] = feat[2, :, cs].astype(bf16)


def pair_chunk(source, offset, flow, wide, left, pot_ref, shift):
    width = wide.shape[1]
    for j in range(width // LANES):
        cs = slice(offset + LANES * j, offset + LANES * j + LANES)
        source_rows = [jnp.broadcast_to(source[c : c + 1, cs], (ROWS, LANES)) for c in (0, 1, 2, 6)]
        for rb in range(width // ROWS):
            rs = slice(rb * ROWS, rb * ROWS + ROWS)
            dx, dy, dz = (source_rows[c] - wide[c, rs, :] for c in range(3))
            inverse = lax.rsqrt(((dx * dx + soften) + dy * dy) + dz * dz)
            inv_sq = inverse * inverse
            weighted = source_rows[3] * inverse
            pot_ref[rs, :] += weighted
            cube = weighted * inv_sq
            if shift is not None and rb * ROWS // LANES == j:
                here = lax.broadcasted_iota(jnp.int32, (ROWS, LANES), 0) + (rb * ROWS - j * LANES + shift)
                there = lax.broadcasted_iota(jnp.int32, (ROWS, LANES), 1)
                cube = jnp.where(here == there, 0.0, cube)
            radial = cube * (flow[rs, LANES * j : LANES * j + LANES] * inv_sq)
            parts = (
                cube,
                cube - cube.astype(bf16).astype(f32),
                radial,
                radial - radial.astype(bf16).astype(f32),
            )
            for i, x in enumerate(parts):
                left[rs, i * width + LANES * j : i * width + LANES * j + LANES] = x


def add_chunk(left, right, sum_ref):
    sum_ref[...] += lax.dot_general(left[...].astype(bf16), right, BOTH_MINOR, preferred_element_type=f32)


def pair_block(source, wide, near_feat, sum_ref, pot_ref, right, far_feat, left, flow, own_block):
    width = wide.shape[1]
    chunks = right.shape[0]
    rank = lax.axis_index("ia")
    mine = near_feat[...].astype(bf16)

    def set_flow(k):
        flow[k % 2] = jnp.dot(mine, far_feat[k], preferred_element_type=f32)

    set_flow(0)
    for k in range(chunks):
        if k + 1 < chunks:
            set_flow(k + 1)
        if k:
            add_chunk(left.at[(k - 1) % 2], right[k - 1], sum_ref)
        shift = jnp.where(rank == k, 0, width) if own_block else None
        pair_chunk(source, k * width, flow.at[k % 2], wide, left.at[k % 2], pot_ref, shift)
    add_chunk(left.at[(chunks - 1) % 2], right[chunks - 1], sum_ref)


def near_kernel(src_ref, own_ref, mid_ref, sum_ref, pot_ref, wide, near_feat, *work):
    feat, right, far_feat, left, flow, rows_ref = work
    set_constants(feat, rows_ref)
    set_targets(own_ref, mid_ref, wide, near_feat, rows_ref)
    set_sources(src_ref, mid_ref, feat, right, far_feat, own_ref.shape[1])
    sum_ref[...] = jnp.zeros(sum_ref.shape, f32)
    pot_ref[...] = jnp.zeros(pot_ref.shape, f32)
    pair_block(src_ref, wide, near_feat, sum_ref, pot_ref, right, far_feat, left, flow, True)


def twin_kernel(count, *refs):
    blocks = refs[:count]
    src_ref, mid_ref, wide, near_feat, sum_in, pot_in = refs[count : count + 6]
    sum_ref, pot_ref, other_sum, other_pot, other_own, other_wide, other_feat = refs[count + 6 : count + 13]
    feat, right, far_feat, left, flow, rows_ref = refs[count + 13 :]
    width = wide.shape[1]
    stars = src_ref.shape[1]
    mine = pl.ds(pl.multiple_of(lax.axis_index("ia") * width, LANES), width)
    other_own[0:8, :] = blocks[-1][:, mine]
    other_own[8:16, :] = blocks[-1][:, stars : stars + width]
    set_constants(feat, rows_ref)
    set_targets(other_own, mid_ref, other_wide, other_feat, rows_ref)
    sum_ref[...] = sum_in[...]
    pot_ref[...] = pot_in[...]
    other_sum[...] = jnp.zeros(other_sum.shape, f32)
    other_pot[...] = jnp.zeros(other_pot.shape, f32)
    for i, block in enumerate((*blocks, src_ref)):
        set_sources(block, mid_ref, feat, right, far_feat, width)
        if i < count:
            pair_block(block, wide, near_feat, sum_ref, pot_ref, right, far_feat, left, flow, False)
        pair_block(
            block, other_wide, other_feat, other_sum, other_pot, right, far_feat, left, flow, i == count - 1
        )


def finish(own_ref, mid_ref, sum_ref, pot_ref, out_ref, cs):
    width = own_ref.shape[1]
    sums = jnp.transpose(sum_ref[...])
    pot = jnp.sum(jnp.transpose(pot_ref[...]), axis=0, keepdims=True)
    near_pos, near_vel = centred(own_ref[0:6, :], mid_ref)
    total = sums[18:19, :]
    new_acc = (sums[0:3, :] - near_pos * total) + sums[3:6, :] + sums[6:9, :]
    drift = (sums[9:12, :] - near_vel * total) + sums[12:15, :] + sums[15:18, :]
    pull = (sums[24:27, :] - near_pos * sums[33:34, :]) + sums[27:30, :] + sums[30:33, :]
    new_jolt = drift - 3.0 * pull
    position, velocity = correct(
        own_ref[0:3, :], own_ref[3:6, :], own_ref[8:11, :], own_ref[11:14, :], own_ref[7:8, :], new_acc, new_jolt
    )
    out_ref[0:3, cs] = position
    out_ref[3:6, cs] = velocity
    out_ref[6:8, cs] = jnp.zeros((2, width), f32)
    out_ref[8:11, cs] = new_acc
    out_ref[11:14, cs] = new_jolt
    out_ref[14:15, cs] = -pot
    out_ref[15:16, cs] = jnp.zeros((1, width), f32)


def last_kernel(count, *refs):
    blocks = refs[:count]
    mid_ref = refs[count]
    sets = (refs[count + 1 : count + 6], refs[count + 6 : count + 11])
    out_ref = refs[count + 11]
    totals = (refs[count + 12 : count + 14], refs[count + 14 : count + 16])
    feat, right, far_feat, left, flow, rows_ref = refs[count + 16 :]
    set_constants(feat, rows_ref)
    for (own_ref, wide, near_feat, sum_in, pot_in), (sum_ref, pot_ref) in zip(sets, totals):
        sum_ref[...] = sum_in[...]
        pot_ref[...] = pot_in[...]
    width = sets[0][0].shape[1]
    for block in blocks:
        set_sources(block, mid_ref, feat, right, far_feat, width)
        for (own_ref, wide, near_feat, sum_in, pot_in), (sum_ref, pot_ref) in zip(sets, totals):
            pair_block(block, wide, near_feat, sum_ref, pot_ref, right, far_feat, left, flow, False)
    for i, ((own_ref, wide, near_feat, sum_in, pot_in), (sum_ref, pot_ref)) in enumerate(zip(sets, totals)):
        finish(own_ref, mid_ref, sum_ref, pot_ref, out_ref, slice(i * width, i * width + width))


def pick_kernel(ia_bits, ja_bits, width, first_slot, last, refs):
    table_ref, local_ref, owner_ref = refs[:3]
    before = refs[3:-2]
    state_ref, forces_ref = refs[-2:]
    count = local_ref.shape[0]
    per = width // LANES
    my_ja = lax.axis_index("ja")
    my_ia = lax.axis_index("ia")
    for b in range(count // LANES):
        cs = slice(b * LANES, b * LANES + LANES)
        local = local_ref[cs].reshape(1, LANES)
        apart_ja = lax.bitwise_xor(owner_ref[cs].reshape(1, LANES), my_ja)
        apart_ia = lax.bitwise_xor(local // width, my_ia)
        step = lax.bitwise_and(apart_ja, (1 << (ja_bits - 1)) - 1)
        flips = apart_ia + (step != 0).astype(jnp.int32)
        for i in range(1, ia_bits):
            flips = flips + lax.shift_right_logical(apart_ia, i)
        slot = step + step + lax.shift_right_logical(apart_ja, ja_bits - 1)
        slot = slot + lax.shift_left(lax.shift_right_logical(apart_ia, 1), ja_bits)
        slot = slot + lax.shift_left(lax.bitwise_and(flips, 1), ja_bits + ia_bits - 1)
        within = lax.rem(local, width)
        piece = jnp.broadcast_to((slot - first_slot) * per + within // LANES, (8, LANES))
        lane = jnp.broadcast_to(lax.rem(within, LANES), (8, LANES))
        state = before[0][:, cs] if before else jnp.zeros((8, LANES), f32)
        forces = before[1][:, cs] if before else jnp.zeros((8, LANES), f32)
        for t in range(table_ref.shape[1] // LANES):
            hit = piece == t
            ts = slice(t * LANES, t * LANES + LANES)
            state = jnp.where(hit, jnp.take_along_axis(table_ref[0:8, ts], lane, axis=1), state)
            forces = jnp.where(hit, jnp.take_along_axis(table_ref[8:16, ts], lane, axis=1), forces)
        state_ref[:, cs] = state[0 : state_ref.shape[0], :]
        forces_ref[:, cs] = forces[0 : forces_ref.shape[0], :]


def shape_of(*dims):
    return jax.ShapeDtypeStruct(dims, f32)


def all_stars(nj, ni, pos_vel, acc_jerk, mass, age, active_local, active_owner):
    stars = mass.shape[0]
    width = stars // ni
    chunks = stars // width
    ja_bits = nj.bit_length() - 1
    ia_bits = ni.bit_length() - 1

    def exchange(x, dj, di):
        pairs = [(j * ni + i, (j ^ dj) * ni + (i ^ di)) for j in range(nj) for i in range(ni)]
        return lax.ppermute(x, ("ja", "ia"), pairs)

    twin = nj // 2
    src, long, own, mid = pl.pallas_call(
        predict_kernel,
        out_shape=(shape_of(8, stars), shape_of(8, stars + width), shape_of(16, width), shape_of(8, LANES)),
        in_specs=[pl.BlockSpec(memory_space=pltpu.HBM)] * 4,
        out_specs=(VMEM,) * 4,
        scratch_shapes=[
            pltpu.VMEM((6, stars), f32),
            pltpu.VMEM((6, stars), f32),
            pltpu.VMEM((1, stars), f32),
            pltpu.VMEM((1, stars), f32),
            pltpu.SemaphoreType.DMA((4,)),
        ],
        compiler_params=PARAMS,
        name="predict",
    )(*(pltpu.with_memory_space_constraint(x, pltpu.HBM) for x in (pos_vel, acc_jerk, mass[None, :], age[None, :])))
    others = [exchange(long if d == twin else src, d, 1) for d in range(1, nj)]
    scratch = [
        pltpu.VMEM((3, COLS, stars), f32),
        pltpu.VMEM((chunks, COLS, 4 * width), bf16),
        pltpu.VMEM((chunks, COLS, width), bf16),
        pltpu.VMEM((2, width, 4 * width), f32),
        pltpu.VMEM((2, width, width), f32),
        pltpu.VMEM((COLS, width), f32),
    ]
    held = (shape_of(width, COLS), shape_of(width, LANES))
    aims = (shape_of(3, width, LANES), shape_of(width, COLS))

    def call(kernel, name, blocks, out_shape, more, args):
        single = not isinstance(out_shape, tuple)
        return pl.pallas_call(
            kernel,
            out_shape=out_shape,
            in_specs=[VMEM] * len(args),
            out_specs=VMEM if single else (VMEM,) * len(out_shape),
            scratch_shapes=more + scratch,
            compiler_params=PARAMS,
            cost_estimate=pl.CostEstimate(
                flops=blocks * 40 * width * stars, transcendentals=blocks * width * stars, bytes_accessed=400000
            ),
            name=name,
        )(*args)

    sums, pot, wide, feat = call(near_kernel, "near", 1, held + aims, [], (src, own, mid))
    sums, pot, other_sums, other_pot, other_own, other_wide, other_feat = call(
        lambda *refs: twin_kernel(twin, *refs),
        "twin",
        2 * twin + 1,
        held + held + (shape_of(16, width),) + aims,
        [],
        (*others[:twin], src, mid, wide, feat, sums, pot),
    )
    block = call(
        lambda *refs: last_kernel(nj - 1 - twin, *refs),
        "last",
        2 * (nj - 1 - twin),
        shape_of(16, 2 * width),
        [pltpu.VMEM(x.shape, f32) for x in held + held],
        (*others[twin:], mid, own, wide, feat, sums, pot, other_own, other_wide, other_feat, other_sums, other_pot),
    )
    count = active_local.shape[0]

    def pick(table, first_slot, before, last=False):
        return pl.pallas_call(
            lambda *refs: pick_kernel(ia_bits, ja_bits, width, first_slot, last, refs),
            out_shape=(shape_of(6 if last else 8, count), shape_of(7 if last else 8, count)),
            in_specs=[VMEM] * (3 + len(before)),
            out_specs=(VMEM, VMEM),
            compiler_params=PARAMS,
            cost_estimate=pl.CostEstimate(flops=count * table.shape[1], transcendentals=0, bytes_accessed=400000),
            name="pick",
        )(table, active_local, active_owner, *before)

    table = jnp.concatenate([block, *(exchange(block, d, 1) for d in range(1, twin))], axis=1)
    half = 1 << (ja_bits + ia_bits - 1)
    tables = [(0, table)]
    came = [(half, exchange(table, 0, 1))]
    for bit in range(1, ia_bits):
        for slot, there in list(tables):
            fresh = exchange(there, 0, (1 << bit) + 1)
            new_slot = slot + (nj << (bit - 1))
            tables.append((new_slot, fresh))
            came.append((half + new_slot, exchange(fresh, 0, 1)))
    order = [tables[0], came[0]]
    for pair in zip(tables[1:], came[1:]):
        order.extend(pair)
    found = ()
    for i, (slot, there) in enumerate(order):
        found = pick(there, slot, found, i == len(order) - 1)
    return found


def solution(mesh):
    nj = mesh.shape["ja"]
    ni = mesh.shape["ia"]

    def local(pos_vel, acc_jerk, mass, age, active_local, active_owner):
        stars = mass.shape[0]
        width = stars // ni
        fits = (
            nj & (nj - 1) == 0
            and ni & (ni - 1) == 0
            and 1 < nj <= 8
            and ni > 1
            and stars % ni == 0
            and width % LANES == 0
            and width <= 256
            and active_local.shape[0] % LANES == 0
            and stars * nj <= active_local.shape[0] * ni
        )
        args = (pos_vel, acc_jerk, mass, age, active_local, active_owner)
        return all_stars(nj, ni, *args) if fits else general(*args)

    return jax.shard_map(
        local,
        mesh=mesh,
        in_specs=(
            P(None, ("grp", "ja")),
            P(None, ("grp", "ja")),
            P(("grp", "ja")),
            P(("grp", "ja")),
            P(("grp", "ia")),
            P(("grp", "ia")),
        ),
        out_specs=(P(None, ("grp", "ia")), P(None, ("grp", "ia"))),
        check_vma=False,
    )
```
